32 devices in a mesh: pipe: 2 (over x), expert: 16 (over z, y, core).
Axes of the slice: x: 2, y: 2, z: 4, core: 2. Of those that a mesh axis runs over, the one named last changes fastest.
Arguments:
- fwd_input: bfloat16 [2, 1024, 3584], P('pipe', 'expert'), may hold values from -6 to 6
- fwd_routes: int32 [2, 1024, 2], P('pipe', 'expert'), may hold values from 0 to 3, all different within a row; in each aligned block of 64 rows (0 to 63, 64 to 127, ..., all dimensions but the last counted through in order) at most 40 rows name the same one
- fwd_gates: bfloat16 [2, 1024, 2], P('pipe', 'expert'), may hold values from 0.19921875 to 1
- bwd_input: bfloat16 [2, 1024, 3584], P('pipe', 'expert'), may hold values from -6 to 6
- bwd_routes: int32 [2, 1024, 2], P('pipe', 'expert'), may hold values from 0 to 3, all different within a row; in each aligned block of 64 rows (0 to 63, 64 to 127, ..., all dimensions but the last counted through in order) at most 40 rows name the same one
- bwd_gates: bfloat16 [2, 1024, 2], P('pipe', 'expert'), may hold values from 0.19921875 to 1
- out_grad: bfloat16 [2, 1024, 3584], P('pipe', 'expert'), may hold values from -12 to 12
- norm_gain: float32 [2, 3584], P('pipe'), may hold values from 0.25 to 1.75
- gate_weight: bfloat16 [2, 3584, 4096], P('pipe', None, 'expert'), may hold values from -0.09375 to 0.09375
- up_weight: bfloat16 [2, 3584, 4096], P('pipe', None, 'expert'), may hold values from -0.09375 to 0.09375
- down_weight: bfloat16 [2, 4096, 3584], P('pipe', 'expert'), may hold values from -0.1875 to 0.1875
Outputs:
- act_next: bfloat16 [2, 1024, 3584], P('pipe', 'expert')
- grad_prev: bfloat16 [2, 1024, 3584], P('pipe', 'expert')
- gate_grad: float32 [2, 1024, 2], P('pipe', 'expert')
- gain_grad: float32 [2, 3584], P('pipe')
- grad_gate_weight: bfloat16 [2, 3584, 4096], P('pipe', None, 'expert')
- grad_up_weight: bfloat16 [2, 3584, 4096], P('pipe', None, 'expert')
- grad_down_weight: bfloat16 [2, 4096, 3584], P('pipe', 'expert')
The draws below stay inside these ranges and needn't reach their ends.
Inputs may be any that keep to these rules, and one draw needn't show every extreme that they name: `fwd_routes`: each row names 2 different experts. In the 64 rows of one device (aligned blocks of the flattened rows) no expert is named by more than 40 rows, a bound that some block reaches. `bwd_routes`: each row names 2 different experts. In the 64 rows of one device (aligned blocks of the flattened rows) no expert is named by more than 40 rows, a bound that some block reaches.
All inputs are finite; a program needn't handle non-finite values.
Results may differ from the reference program's by a relative error of at most 0.008.
Values may be sent and summed in bfloat16 or wider, within the bound.
No kernel may reach another device: no remote copies, remote signals or barrier semaphores. Data moves between devices by JAX's collectives and lax.ppermute only.
A program may use at most 128 MiB of HBM per device.

```python
import math
import jax
import jax.numpy as jnp
import numpy as np
from jax import lax

MODEL_DIM = 3584
FF = 1024
UNIT_SPLIT_COUNT = 4
TOP = 2
TOK_DEV = 64
EXPERTS = 4
CAP = 40
TOKENS = 1024
N_PIPE = 2
N_EXPERT = 16


def draw_out_grad(key, part):
    first_key = jax.random.fold_in(key, 11)
    second_key = jax.random.fold_in(key, 12)
    base = jax.random.normal(first_key, (N_PIPE, TOKENS, MODEL_DIM), jnp.float32)
    position = jnp.arange(TOKENS, dtype=jnp.float32) / TOKENS
    rough = jnp.exp(jax.random.uniform(second_key, (N_PIPE, TOKENS, 1), jnp.float32, -0.35, 0.35))
    scale = (1.0 + 2.0 * position)[None, :, None] * rough
    return jnp.clip(base * scale, -12.0, 12.0).astype(jnp.bfloat16)


def shard_levels(own_key, extent, split, least, top_value):
    factor_of, own = 1.0, jax.random.fold_in(own_key, 6)
    for dim, blocks in split:
        steps = jnp.exp(jax.random.uniform(jax.random.fold_in(own, dim), (blocks,), jnp.float32, least / len(split), top_value / len(split)))
        factor_of = factor_of * jnp.repeat(steps, extent[dim] // blocks).reshape([-1 if axis == dim else 1 for axis in range(len(extent))])
    return factor_of


def deal_out(key, own, number, rows, count, top, reach, skew):
    order = jax.random.permutation(key, count)
    crowded, usual = load_shares(count, rows * top, reach, skew, True), load_shares(count, rows * top, reach, skew, False)
    places = jnp.arange(count)

    def named(sizes, rotation):
        used = int((sizes > 0).sum())
        fixed = max(1, used // 4)
        moved = fixed + (places - fixed + rotation * (used - fixed)) % max(1, count - fixed)
        return jnp.zeros((count,), jnp.int32).at[order[jnp.where(places < fixed, places, moved)]].set(jnp.asarray(sizes, jnp.int32))

    sizes = jnp.where(number % 4 == 0, named(crowded, number // 4), named(usual, number - number // 4 - 1))
    mixed = jax.random.permutation(jax.random.fold_in(own, 3), count)
    source_of, sink = mixed[0:count // 2 * 2:2], mixed[1:count // 2 * 2:2]
    room = jnp.minimum(sizes[source_of] - 1, reach - sizes[sink]) // 2
    room = jnp.where((source_of == order[0]) | (sink == order[0]) | (sizes[sink] == 0), 0, jnp.maximum(room, 0))
    moved = jax.random.randint(jax.random.fold_in(own, 4), (count // 2,), 0, 1 << 20) % (room + 1)
    sizes = sizes.at[source_of].add(-moved).at[sink].add(moved)
    members = jnp.searchsorted(jnp.cumsum(sizes), jnp.arange(rows * top), side="right").astype(jnp.int32)
    listing = members.reshape(top, rows).T
    listing = listing[jax.random.permutation(jax.random.fold_in(own, 1), rows)]
    rotation = jax.random.randint(jax.random.fold_in(own, 2), (rows, 1), 0, top)
    return jnp.take_along_axis(listing, (jnp.arange(top)[None, :] + rotation) % top, axis=1)


def load_shares(number_of, total, limit, lean, full):
    weights = [(1 << 20) // math.isqrt(standing ** lean) + 1 for standing in range(1, number_of + 1)]
    largest = limit if full else min(limit, max(-(-total // number_of), total * weights[0] // sum(weights)))
    least = 1 if total - largest >= number_of - 1 else 0
    holding, surplus = [largest] + [least] * (number_of - 1), total - largest - least * (number_of - 1)
    while surplus > 0:
        candidates = [i for i in range(1, number_of) if holding[i] < largest] or [i for i in range(1, number_of) if holding[i] < limit]
        pool, remaining = sum([weights[i] for i in candidates]), surplus
        for i in candidates:
            extra = min(limit - holding[i], max(1, remaining * weights[i] // pool), surplus)
            holding[i] = holding[i] + extra
            surplus = surplus - extra
    return np.array(holding)


def centred(stream_key, shape, width, bound, split=(), held_as=jnp.bfloat16):
    values = jax.random.normal(stream_key, shape, jnp.float32) * width
    if len(split) > 0:
        values = shard_levels(stream_key, shape, split, -0.22, 0.18) * values
    return jnp.clip(values, min=-bound, max=bound).astype(held_as)


def setup_inputs(seed: int = 0) -> dict:
    keys = jax.random.split(jax.random.key(seed), 12)
    fwd_input = centred(keys[0], (N_PIPE, TOKENS, MODEL_DIM), 1.0, 6.0, ((0, 2), (1, 16)))
    fwd_routes_keys = jax.random.split(jax.random.fold_in(keys[1], 1), N_PIPE * TOKENS // TOK_DEV)
    fwd_routes_turns = jax.random.permutation(jax.random.fold_in(keys[1], 3), N_PIPE * TOKENS // TOK_DEV)
    fwd_routes = jax.vmap(lambda own, number: deal_out(jax.random.fold_in(keys[1], 2), own, number, TOK_DEV, EXPERTS, TOP, CAP, 2))(fwd_routes_keys, fwd_routes_turns).reshape((N_PIPE, TOKENS, TOP))
    fwd_gates = jnp.clip(0.19921875 + 0.80078125 * jax.random.uniform(keys[2], (N_PIPE, TOKENS, TOP), jnp.float32) ** shard_levels(keys[2], (N_PIPE, TOKENS, TOP), ((0, 2), (1, 16)), -0.2, 0.2), 0.19921875, 1.0).astype(jnp.bfloat16)
    bwd_input = centred(keys[3], (N_PIPE, TOKENS, MODEL_DIM), 1.0, 6.0, ((0, 2), (1, 16)))
    bwd_routes_keys = jax.random.split(jax.random.fold_in(keys[4], 1), N_PIPE * TOKENS // TOK_DEV)
    bwd_routes_turns = jax.random.permutation(jax.random.fold_in(keys[4], 3), N_PIPE * TOKENS // TOK_DEV)
    bwd_routes = jax.vmap(lambda own, number: deal_out(jax.random.fold_in(keys[4], 2), own, number, TOK_DEV, EXPERTS, TOP, CAP, 2))(bwd_routes_keys, bwd_routes_turns).reshape((N_PIPE, TOKENS, TOP))
    bwd_gates = jnp.clip(0.19921875 + 0.80078125 * jax.random.uniform(keys[5], (N_PIPE, TOKENS, TOP), jnp.float32) ** shard_levels(keys[5], (N_PIPE, TOKENS, TOP), ((0, 2), (1, 16)), -0.2, 0.2), 0.19921875, 1.0).astype(jnp.bfloat16)
    out_grad = draw_out_grad(jax.random.fold_in(keys[11], 71), 0)
    norm_gain = jnp.clip(1.0 + 0.15 * jax.random.normal(keys[7], (N_PIPE, MODEL_DIM), jnp.float32), 0.25, 1.75)
    gate_weight = centred(keys[8], (N_PIPE, MODEL_DIM, EXPERTS * FF), MODEL_DIM ** -0.5, 0.09375, ((0, 2), (2, 16)))
    up_weight = centred(keys[9], (N_PIPE, MODEL_DIM, EXPERTS * FF), MODEL_DIM ** -0.5, 0.09375, ((0, 2), (2, 16)))
    down_weight = centred(keys[10], (N_PIPE, EXPERTS * FF, MODEL_DIM), FF ** -0.5, 0.1875, ((0, 2), (1, 16)))
    return dict(fwd_input=fwd_input, fwd_routes=fwd_routes, fwd_gates=fwd_gates, bwd_input=bwd_input, bwd_routes=bwd_routes, bwd_gates=bwd_gates, out_grad=out_grad, norm_gain=norm_gain, gate_weight=gate_weight, up_weight=up_weight, down_weight=down_weight)


epsilon = 1e-06

def normalize(values, gain):
    wide = values.astype(jnp.float32)
    inverse = lax.rsqrt(lax.optimization_barrier(jnp.mean(wide * wide, axis=-1, keepdims=True)) + epsilon)
    normed = wide * inverse
    return ((normed * gain[None, :]).astype(jnp.bfloat16), normed, inverse)

def rounded(values):
    return lax.optimization_barrier(values.astype(jnp.bfloat16)).astype(jnp.float32)

def expert_pairs(route_ids):
    flat = route_ids.reshape(-1).astype(jnp.int32)
    total_pairs = flat.shape[0]
    most_rows = N_EXPERT * CAP
    order = jnp.argsort(flat, stable=True).astype(jnp.int32)
    counts = lax.optimization_barrier(jnp.sum((flat[:, None] == jnp.arange(EXPERTS, dtype=jnp.int32)[None, :]).astype(jnp.int32), axis=0))
    starts = (jnp.cumsum(counts) - counts).astype(jnp.int32)
    padded = jnp.concatenate([order, jnp.full((most_rows,), total_pairs, jnp.int32)])

    def pick(expert_id):
        segment = lax.dynamic_slice(padded, (starts[expert_id],), (most_rows,))
        return jnp.where(jnp.arange(most_rows, dtype=jnp.int32) < counts[expert_id], segment, total_pairs)
    return jax.vmap(pick)(jnp.arange(EXPERTS, dtype=jnp.int32))

def section(inputs):
    fwd_input, fwd_routes, fwd_gates, bwd_input, bwd_routes, bwd_gates, out_grad, gain, gate_weight, up_weight, down_weight = inputs
    fourth_breadth = FF // UNIT_SPLIT_COUNT
    total_pairs = TOKENS * TOP
    fwd_norm, unused_normed, unused_inverse = normalize(fwd_input, gain)
    bwd_norm, bwd_normed, bwd_inverse = normalize(bwd_input, gain)
    zero_row = jnp.zeros((1, MODEL_DIM), jnp.bfloat16)
    fwd_pad = jnp.concatenate([fwd_norm, zero_row], axis=0)
    bwd_pad = jnp.concatenate([bwd_norm, zero_row], axis=0)
    cot_pad = jnp.concatenate([out_grad, zero_row], axis=0)
    gate_pad = jnp.concatenate([bwd_gates.reshape(-1), jnp.zeros((1,), jnp.bfloat16)])
    fwd_pairs = expert_pairs(fwd_routes)
    bwd_pairs = expert_pairs(bwd_routes)
    gate_cube = gate_weight.reshape(MODEL_DIM, EXPERTS, FF)
    up_cube = up_weight.reshape(MODEL_DIM, EXPERTS, FF)
    down_cube = down_weight.reshape(EXPERTS, FF, MODEL_DIM)

    def one_expert(expert_id):
        gate_matrix = lax.dynamic_index_in_dim(gate_cube, expert_id, 1, keepdims=False)
        up_matrix = lax.dynamic_index_in_dim(up_cube, expert_id, 1, keepdims=False)
        weight_down = lax.dynamic_index_in_dim(down_cube, expert_id, 0, keepdims=False)
        rows_fwd = fwd_pad[fwd_pairs[expert_id] // TOP]
        pre_gate = jnp.dot(rows_fwd, gate_matrix, preferred_element_type=jnp.float32)
        pre_up = jnp.dot(rows_fwd, up_matrix, preferred_element_type=jnp.float32)
        live_inner_units = (pre_gate * jax.nn.sigmoid(pre_gate) * pre_up).astype(jnp.bfloat16)
        specialist_places = live_inner_units.shape[0]
        lowering_fragments = weight_down.astype(jnp.float32).reshape(UNIT_SPLIT_COUNT, fourth_breadth, MODEL_DIM)
        result_fragments = jnp.einsum('igf,gfl->gil', live_inner_units.astype(jnp.float32).reshape(specialist_places, UNIT_SPLIT_COUNT, fourth_breadth), lowering_fragments)
        out_fwd = lax.optimization_barrier(jnp.sum(rounded(result_fragments), axis=0))
        rows_bwd = bwd_pad[bwd_pairs[expert_id] // TOP]
        rows_cot = cot_pad[bwd_pairs[expert_id] // TOP]
        row_gate = gate_pad[bwd_pairs[expert_id]].astype(jnp.float32)[:, None]
        pre_gate_b = jnp.dot(rows_bwd, gate_matrix, preferred_element_type=jnp.float32)
        pre_up_b = jnp.dot(rows_bwd, up_matrix, preferred_element_type=jnp.float32)
        sigma = jax.nn.sigmoid(pre_gate_b)
        swish = pre_gate_b * sigma
        active_b = (swish * pre_up_b).astype(jnp.bfloat16)
        upstream = jnp.dot(rows_cot, weight_down.T, preferred_element_type=jnp.float32)
        gate_parts = rounded(lax.optimization_barrier(jnp.sum((active_b.astype(jnp.float32) * upstream).reshape(specialist_places, UNIT_SPLIT_COUNT, fourth_breadth), axis=-1)))
        gate_term = lax.optimization_barrier(jnp.sum(gate_parts, axis=-1))
        scaled = (row_gate * rows_cot.astype(jnp.float32)).astype(jnp.bfloat16)
        grad_down = jnp.dot(active_b.T, scaled, preferred_element_type=jnp.float32).astype(jnp.bfloat16)
        act_grad = row_gate * upstream
        gate_preact_gradient = (act_grad * pre_up_b * sigma * (1.0 + pre_gate_b * (1.0 - sigma))).astype(jnp.bfloat16)
        up_preact_gradient = (act_grad * swish).astype(jnp.bfloat16)
        grad_gate = jnp.dot(rows_bwd.T, gate_preact_gradient, preferred_element_type=jnp.float32).astype(jnp.bfloat16)
        grad_up = jnp.dot(rows_bwd.T, up_preact_gradient, preferred_element_type=jnp.float32).astype(jnp.bfloat16)
        backward_pieces = jnp.einsum('jnb,hnb->njh', gate_preact_gradient.astype(jnp.float32).reshape(specialist_places, UNIT_SPLIT_COUNT, fourth_breadth), gate_matrix.astype(jnp.float32).reshape(MODEL_DIM, UNIT_SPLIT_COUNT, fourth_breadth))
        backward_pieces = backward_pieces + jnp.einsum('jnb,hnb->njh', up_preact_gradient.astype(jnp.float32).reshape(specialist_places, UNIT_SPLIT_COUNT, fourth_breadth), up_matrix.astype(jnp.float32).reshape(MODEL_DIM, UNIT_SPLIT_COUNT, fourth_breadth))
        row_grad = lax.optimization_barrier(jnp.sum(rounded(backward_pieces), axis=0))
        return (out_fwd, row_grad, gate_term, grad_gate, grad_up, grad_down)
    out_fwd, row_grad, gate_term, grad_gate, grad_up, grad_down = lax.map(one_expert, jnp.arange(EXPERTS, dtype=jnp.int32))
    fwd_value = jnp.zeros((total_pairs + 1, MODEL_DIM), jnp.float32).at[fwd_pairs.reshape(-1)].add(out_fwd.reshape(-1, MODEL_DIM))
    fwd_value = fwd_value[:total_pairs].reshape(TOKENS, TOP, MODEL_DIM)
    mixed = (fwd_input.astype(jnp.float32) + lax.optimization_barrier(jnp.sum(fwd_gates.astype(jnp.float32)[:, :, None] * fwd_value, axis=1))).astype(jnp.bfloat16)
    bwd_value = jnp.zeros((total_pairs + 1, MODEL_DIM), jnp.float32).at[bwd_pairs.reshape(-1)].add(row_grad.reshape(-1, MODEL_DIM))
    norm_grad = lax.optimization_barrier(jnp.sum(bwd_value[:total_pairs].reshape(TOKENS, TOP, MODEL_DIM), axis=1))
    gate_grad = jnp.zeros((total_pairs + 1,), jnp.float32).at[bwd_pairs.reshape(-1)].add(gate_term.reshape(-1))
    gate_grad = gate_grad[:total_pairs].reshape(TOKENS, TOP)
    gain_grad = lax.optimization_barrier(jnp.sum(norm_grad * bwd_normed, axis=0))
    scaled_grad = norm_grad * gain[None, :]
    input_grad = (out_grad.astype(jnp.float32) + bwd_inverse * (scaled_grad - bwd_normed * lax.optimization_barrier(jnp.mean(scaled_grad * bwd_normed, axis=-1, keepdims=True)))).astype(jnp.bfloat16)
    grad_gate_full = jnp.transpose(grad_gate, (1, 0, 2)).reshape(MODEL_DIM, EXPERTS * FF)
    grad_up_full = jnp.transpose(grad_up, (1, 0, 2)).reshape(MODEL_DIM, EXPERTS * FF)
    grad_down_full = grad_down.reshape(EXPERTS * FF, MODEL_DIM)
    return (mixed, input_grad, gate_grad, gain_grad, grad_gate_full, grad_up_full, grad_down_full)

def reference(fwd_input, fwd_routes, fwd_gates, bwd_input, bwd_routes, bwd_gates, out_grad, norm_gain, gate_weight, up_weight, down_weight):
    results = lax.map(section, (fwd_input, fwd_routes, fwd_gates, bwd_input, bwd_routes, bwd_gates, out_grad, norm_gain, gate_weight, up_weight, down_weight))
    mixed, input_grad, gate_grad, gain_grad, grad_gate_full, grad_up_full, grad_down_full = results
    act_next = jnp.concatenate([jnp.zeros_like(mixed[:1]), mixed[:-1]], axis=0)
    grad_prev = jnp.concatenate([input_grad[1:], jnp.zeros_like(input_grad[:1])], axis=0)
    return (act_next, grad_prev, gate_grad, gain_grad, grad_gate_full, grad_up_full, grad_down_full)
```

```python
import functools

import jax
import jax.numpy as jnp
from jax import lax
from jax.experimental import pallas as pl
from jax.experimental.pallas import tpu as pltpu
from jax.sharding import PartitionSpec as P

UNIT_SPLIT_COUNT = 4
EPSILON = 1e-06
LANES = 128
BF16 = jnp.bfloat16
F32 = jnp.float32


def chunk_of(width):
    for size in (512, 256, 128):
        if width % size == 0:
            return size
    return width


def swap(value, mask):
    count = lax.axis_size("expert")
    return lax.ppermute(value, "expert", [(source, source ^ mask) for source in range(count)])


def along_pipe(value, steps):
    count = lax.axis_size("pipe")
    first, last = (max(0, -steps), min(count, count - steps))
    return lax.ppermute(value, "pipe", [(source, source + steps) for source in range(first, last)])


def dot_rows(left, right):
    return lax.dot_general(left, right, (((0,), (0,)), ((), ())), preferred_element_type=F32)


def dot_cols(left, right):
    return lax.dot_general(left, right, (((1,), (1,)), ((), ())), preferred_element_type=F32)


def dot(left, right):
    return lax.dot_general(left, right, (((1,), (0,)), ((), ())), preferred_element_type=F32)


def members(plane, routes, experts):
    tokens = routes.shape[1]
    height = -(-experts // 8) * 8
    expert = lax.broadcasted_iota(jnp.int32, (height, tokens), 0) ^ plane
    named = [routes[k : k + 1, :] == expert for k in range(routes.shape[0])]
    chosen = functools.reduce(jnp.logical_or, named)
    earlier = lax.broadcasted_iota(jnp.int32, (tokens, tokens), 0) < lax.broadcasted_iota(
        jnp.int32, (tokens, tokens), 1
    )
    rank = dot(chosen.astype(F32).astype(BF16), earlier.astype(F32).astype(BF16)).astype(jnp.int32)
    return chosen, rank, named


def slots_of(chosen, rank, d, slots):
    tokens = rank.shape[1]
    place = lax.broadcasted_iota(jnp.int32, (slots, tokens), 0)
    row = jnp.where(chosen[d : d + 1, :], rank[d : d + 1, :], -1)
    return place == row


def norm_factor(values_ref, chunk):
    tokens, width = values_ref.shape

    def add(i, total):
        part = values_ref[:, pl.ds(pl.multiple_of(i * chunk, chunk), chunk)].astype(F32)
        return total + jnp.sum(part * part, axis=1, keepdims=True)

    total = lax.fori_loop(0, width // chunk, add, jnp.zeros((tokens, 1), F32))
    return lax.rsqrt(total * (1.0 / width) + EPSILON)


def select_norm_kernel(experts, slots, plane_ref, routes_ref, values_ref, gain_ref, *out_refs):
    width = values_ref.shape[1]
    chunk = chunk_of(width)
    chosen, rank, _ = members(plane_ref[0], routes_ref[...], experts)
    picks = jnp.concatenate(
        [slots_of(chosen, rank, d, slots).astype(F32) for d in range(experts)], axis=0
    ).astype(BF16)
    inverse = norm_factor(values_ref, chunk)

    def step(i, carry):
        cols = pl.ds(pl.multiple_of(i * chunk, chunk), chunk)
        normed = values_ref[:, cols].astype(F32) * inverse
        rows = dot(picks, (normed * gain_ref[:, cols]).astype(BF16)).astype(BF16)
        for d in range(experts):
            out_refs[d][0, :, cols] = rows[d * slots : (d + 1) * slots]
        return carry

    lax.fori_loop(0, width // chunk, step, 0)


def select_both_kernel(
    experts, slots, plane_ref, routes_ref, gates_ref, values_ref, gain_ref, cot_ref, *out_refs
):
    width = values_ref.shape[1]
    chunk = chunk_of(width)
    chosen, rank, named = members(plane_ref[0], routes_ref[...], experts)
    gates = gates_ref[...].astype(F32)
    gate_of = sum(jnp.where(hit, gates[k : k + 1, :], 0.0) for k, hit in enumerate(named))
    hits = [slots_of(chosen, rank, d, slots) for d in range(experts)]
    picks = jnp.concatenate([hit.astype(F32) for hit in hits], axis=0).astype(BF16)
    gate_col = jnp.concatenate(
        [
            jnp.sum(jnp.where(hit, gate_of[d : d + 1, :], 0.0), axis=1, keepdims=True)
            for d, hit in enumerate(hits)
        ],
        axis=0,
    )
    inverse = norm_factor(values_ref, chunk)

    def step(i, carry):
        cols = pl.ds(pl.multiple_of(i * chunk, chunk), chunk)
        normed = values_ref[:, cols].astype(F32) * inverse
        rows = dot(picks, (normed * gain_ref[:, cols]).astype(BF16)).astype(BF16)
        scaled = (dot(picks, cot_ref[:, cols]) * gate_col).astype(BF16)
        for d in range(experts):
            out_refs[d][0, :, cols] = rows[d * slots : (d + 1) * slots]
            out_refs[d][1, :, cols] = scaled[d * slots : (d + 1) * slots]
        return carry

    lax.fori_loop(0, width // chunk, step, 0)


def forward_kernel(rows_ref, gate_ref, up_ref, down_ref, out_ref):
    rows = rows_ref[0]
    pre_gate = dot(rows, gate_ref[...])
    pre_up = dot(rows, up_ref[...])
    act = (pre_gate * jax.nn.sigmoid(pre_gate) * pre_up).astype(BF16)
    width = out_ref.shape[1]
    chunk = chunk_of(width)

    def step(i, carry):
        cols = pl.ds(pl.multiple_of(i * chunk, chunk), chunk)
        out_ref[:, cols] = dot(act, down_ref[:, cols]).astype(BF16)
        return carry

    lax.fori_loop(0, width // chunk, step, 0)


def backward_kernel(
    rows_ref, gate_ref, up_ref, down_ref, out_ref, act_ref, gate_grad_ref, up_grad_ref, gain_ref
):
    width = gain_ref.shape[1]
    chunk = chunk_of(width)
    pre_gate = dot(rows_ref[0], gate_ref[...])
    pre_up = dot(rows_ref[0], up_ref[...])
    upstream = dot_cols(rows_ref[1], down_ref[...])
    sigma = jax.nn.sigmoid(pre_gate)
    swish = pre_gate * sigma
    act = (swish * pre_up).astype(BF16)
    act_ref[...] = act
    gate_grad = (upstream * pre_up * sigma * (1.0 + pre_gate * (1.0 - sigma))).astype(BF16)
    up_grad = (upstream * swish).astype(BF16)
    gate_grad_ref[...] = gate_grad
    up_grad_ref[...] = up_grad
    term = jnp.sum(act.astype(F32) * upstream, axis=1, keepdims=True)
    high = term.astype(BF16).astype(F32)
    lane = lax.broadcasted_iota(jnp.int32, (term.shape[0], LANES), 1)
    out_ref[:, width:] = jnp.where(lane < LANES // 2, high, term - high).astype(BF16)

    def step(i, carry):
        cols = pl.ds(pl.multiple_of(i * chunk, chunk), chunk)
        grads = dot_cols(gate_grad, gate_ref[cols, :]) + dot_cols(up_grad, up_ref[cols, :])
        out_ref[:, cols] = grads.astype(BF16)
        gain_ref[:, cols] = jnp.sum(
            grads * rows_ref[0, :, cols].astype(F32), axis=0, keepdims=True
        )
        return carry

    lax.fori_loop(0, width // chunk, step, 0)


def weight_kernel(
    own_ref, other_ref, act_own, act_other, gate_own, gate_other, up_own, up_other,
    grad_gate_ref, grad_up_ref, grad_down_ref,
):
    own, other = own_ref[0], other_ref[0]
    grad_gate_ref[...] = (dot_rows(own, gate_own[...]) + dot_rows(other, gate_other[...])).astype(
        BF16
    )
    grad_up_ref[...] = (dot_rows(own, up_own[...]) + dot_rows(other, up_other[...])).astype(BF16)
    grad_down_ref[...] = (
        dot_rows(act_own[...], own_ref[1]) + dot_rows(act_other[...], other_ref[1])
    ).astype(BF16)


def mixed_kernel(experts, slots, plane_ref, routes_ref, gates_ref, values_ref, *refs):
    block_refs, out_ref = refs[:experts], refs[experts]
    width = values_ref.shape[1]
    chunk = chunk_of(width)
    chosen, rank, named = members(plane_ref[0], routes_ref[...], experts)
    gates = gates_ref[...].astype(F32)
    gate_of = sum(jnp.where(hit, gates[k : k + 1, :], 0.0) for k, hit in enumerate(named))
    weights = [
        jnp.where(slots_of(chosen, rank, d, slots), gate_of[d : d + 1, :], 0.0).astype(BF16)
        for d in range(experts)
    ]

    def step(i, carry):
        cols = pl.ds(pl.multiple_of(i * chunk, chunk), chunk)
        total = sum(dot_rows(weights[d], block_refs[d][:, cols]) for d in range(experts))
        out_ref[:, cols] = (values_ref[:, cols].astype(F32) + total).astype(BF16)
        return carry

    lax.fori_loop(0, width // chunk, step, 0)


def input_grad_kernel(
    experts, slots, plane_ref, routes_ref, gates_ref, values_ref, cot_ref, gain_ref, *refs
):
    block_refs = refs[:experts]
    out_ref, gate_out_ref, scaled_ref = refs[experts:]
    tokens, width = values_ref.shape
    chunk = chunk_of(width)
    chosen, rank, named = members(plane_ref[0], routes_ref[...], experts)
    hits = [slots_of(chosen, rank, d, slots) for d in range(experts)]
    picks = [hit.astype(F32).astype(BF16) for hit in hits]
    inverse = norm_factor(values_ref, chunk)

    terms = []
    for named_k in named:
        total = jnp.zeros((LANES, tokens), F32)
        for d in range(experts):
            mine = jnp.where(named_k[d : d + 1, :], hits[d].astype(F32), 0.0).astype(BF16)
            total = total + dot_rows(block_refs[d][:, width:], mine)
        terms.append(total[0:1] + total[LANES // 2 : LANES // 2 + 1])
    gate_out_ref[...] = jnp.concatenate(terms, axis=0) / gates_ref[...].astype(F32)

    def first(i, carry):
        cols = pl.ds(pl.multiple_of(i * chunk, chunk), chunk)
        grads = sum(dot_rows(picks[d], block_refs[d][:, cols]) for d in range(experts))
        grads = grads * gain_ref[:, cols]
        scaled_ref[:, cols] = grads
        normed = values_ref[:, cols].astype(F32) * inverse
        return carry + jnp.sum(grads * normed, axis=1, keepdims=True)

    mean = lax.fori_loop(0, width // chunk, first, jnp.zeros((tokens, 1), F32)) * (1.0 / width)

    def second(i, carry):
        cols = pl.ds(pl.multiple_of(i * chunk, chunk), chunk)
        normed = values_ref[:, cols].astype(F32) * inverse
        out_ref[:, cols] = (
            cot_ref[:, cols].astype(F32) + inverse * (scaled_ref[:, cols] - normed * mean)
        ).astype(BF16)
        return carry

    lax.fori_loop(0, width // chunk, second, 0)


SMEM_SPEC = pl.BlockSpec(memory_space=pltpu.SMEM)
VMEM_SPEC = pl.BlockSpec(memory_space=pltpu.VMEM)


def call(body, out_shapes, args, name, scratch=(), scalars=0):
    return pl.pallas_call(
        body,
        out_shape=[jax.ShapeDtypeStruct(shape, dtype) for shape, dtype in out_shapes],
        in_specs=[SMEM_SPEC] * scalars + [VMEM_SPEC] * (len(args) - scalars),
        out_specs=[VMEM_SPEC] * len(out_shapes),
        scratch_shapes=list(scratch),
        compiler_params=pltpu.CompilerParams(vmem_limit_bytes=48 << 20),
        name=name,
    )(*args)


def weight_grads(own, other, acts, gates, ups):
    pair, rows, width = own.shape
    units = acts[0].shape[1]
    chunk = chunk_of(width)
    whole = pl.BlockSpec((rows, units), lambda i: (0, 0))
    return pl.pallas_call(
        weight_kernel,
        grid=(width // chunk,),
        out_shape=[
            jax.ShapeDtypeStruct((width, units), BF16),
            jax.ShapeDtypeStruct((width, units), BF16),
            jax.ShapeDtypeStruct((units, width), BF16),
        ],
        in_specs=[pl.BlockSpec((pair, rows, chunk), lambda i: (0, 0, i))] * 2 + [whole] * 6,
        out_specs=[
            pl.BlockSpec((chunk, units), lambda i: (i, 0)),
            pl.BlockSpec((chunk, units), lambda i: (i, 0)),
            pl.BlockSpec((units, chunk), lambda i: (0, i)),
        ],
        compiler_params=pltpu.CompilerParams(vmem_limit_bytes=48 << 20),
        name="weight_grads",
    )(own, other, *acts, *gates, *ups)


def gather_rows(blocks):
    landed = [swap(block, d * UNIT_SPLIT_COUNT) if d else block for d, block in enumerate(blocks)]
    crossed = [swap(block, 2) for block in landed]
    own = jnp.concatenate(landed + crossed, axis=1)
    return own, swap(own, 1)


def return_rows(own, other, experts, slots):
    partner = swap(other, 1)

    def part(index):
        rows = slice(index * slots, (index + 1) * slots)
        return own[rows].astype(F32) + partner[rows].astype(F32)

    crossed = [swap(part(experts + d).astype(BF16), 2) for d in range(experts)]
    sums = [(part(d) + crossed[d].astype(F32)).astype(BF16) for d in range(experts)]
    return [swap(block, d * UNIT_SPLIT_COUNT) if d else block for d, block in enumerate(sums)]


def on_device(
    fwd_input,
    fwd_routes,
    fwd_gates,
    bwd_input,
    bwd_routes,
    bwd_gates,
    out_grad,
    norm_gain,
    gate_weight,
    up_weight,
    down_weight,
):
    devices = lax.axis_size("expert")
    experts = devices // UNIT_SPLIT_COUNT
    tokens, width = fwd_input.shape[1:]
    picks = fwd_routes.shape[2]
    capacity = min(tokens, tokens * picks * 5 // (4 * experts))
    slots = -(-capacity // 8) * 8
    plane = (lax.axis_index("expert") // UNIT_SPLIT_COUNT).astype(jnp.int32).reshape(1)
    gate_matrix, up_matrix, down_matrix = gate_weight[0], up_weight[0], down_weight[0]
    units = gate_matrix.shape[1]
    fwd_ids, bwd_ids = fwd_routes[0].T, bwd_routes[0].T
    fwd_g, bwd_g = fwd_gates[0].T, bwd_gates[0].T

    bwd_blocks = call(
        functools.partial(select_both_kernel, experts, slots),
        [((2, slots, width), BF16)] * experts,
        (plane, bwd_ids, bwd_g, bwd_input[0], norm_gain, out_grad[0]),
        "select_bwd",
        scalars=1,
    )
    fwd_blocks = call(
        functools.partial(select_norm_kernel, experts, slots),
        [((1, slots, width), BF16)] * experts,
        (plane, fwd_ids, fwd_input[0], norm_gain),
        "select_fwd",
        scalars=1,
    )
    bwd_own, bwd_other = gather_rows(bwd_blocks)
    fwd_own, fwd_other = gather_rows(fwd_blocks)
    rows = bwd_own.shape[1]

    def backward(rows_in, name):
        return call(
            backward_kernel,
            [((rows, width + LANES), BF16)] + [((rows, units), BF16)] * 3 + [((1, width), F32)],
            (rows_in, gate_matrix, up_matrix, down_matrix),
            name,
        )

    def forward(rows_in, name):
        return call(
            forward_kernel,
            [((rows, width), BF16)],
            (rows_in, gate_matrix, up_matrix, down_matrix),
            name,
        )[0]

    norm_own, act_own, dgate_own, dup_own, gain_own = backward(bwd_own, "backward_own")
    norm_other, act_other, dgate_other, dup_other, gain_other = backward(bwd_other, "backward_other")
    norm_back = return_rows(norm_own, norm_other, experts, slots)
    out_own = forward(fwd_own, "forward_own")
    out_other = forward(fwd_other, "forward_other")
    out_back = return_rows(out_own, out_other, experts, slots)
    grad_gate, grad_up, grad_down = weight_grads(
        bwd_own, bwd_other, (act_own, act_other), (dgate_own, dgate_other), (dup_own, dup_other)
    )
    gain_sum = gain_own + gain_other
    bit = 1
    while bit < devices:
        gain_sum = gain_sum + swap(gain_sum, bit)
        bit *= 2
    gain_grad = gain_sum / norm_gain

    input_grad, gate_grad = call(
        functools.partial(input_grad_kernel, experts, slots),
        [((tokens, width), BF16), ((picks, tokens), F32)],
        (plane, bwd_ids, bwd_g, bwd_input[0], out_grad[0], norm_gain, *norm_back),
        "input_grad",
        scratch=[pltpu.VMEM((tokens, width), F32)],
        scalars=1,
    )
    mixed = call(
        functools.partial(mixed_kernel, experts, slots),
        [((tokens, width), BF16)],
        (plane, fwd_ids, fwd_g, fwd_input[0], *out_back),
        "mixed",
        scalars=1,
    )[0]
    act_next = along_pipe(mixed, 1)
    grad_prev = along_pipe(input_grad, -1)
    return (
        act_next[None],
        grad_prev[None],
        gate_grad.T[None],
        gain_grad,
        grad_gate[None],
        grad_up[None],
        grad_down[None],
    )


def solution(mesh):
    rows = P("pipe", "expert", None)
    columns = P("pipe", None, "expert")
    return jax.shard_map(
        on_device,
        mesh=mesh,
        in_specs=(rows,) * 7 + (P("pipe", None), columns, columns, rows),
        out_specs=(rows, rows, rows, P("pipe", None), columns, columns, rows),
        check_vma=False,
    )
```

```python
import functools

import jax
import jax.numpy as jnp
from jax import lax
from jax.experimental import pallas as pl
from jax.experimental.pallas import tpu as pltpu
from jax.sharding import PartitionSpec as P

UNIT_SPLIT_COUNT = 4
HINT = pl.CostEstimate(flops=10**11, transcendentals=0, bytes_accessed=1 << 20)
EPSILON = 1e-06
LANES = 128
BF16 = jnp.bfloat16
F32 = jnp.float32


def chunk_of(width):
    for size in (512, 256, 128):
        if width % size == 0:
            return size
    return width


def swap(value, mask):
    count = lax.axis_size("expert")
    return lax.ppermute(value, "expert", [(source, source ^ mask) for source in range(count)])


def along_pipe(value, steps):
    count = lax.axis_size("pipe")
    first, last = (max(0, -steps), min(count, count - steps))
    return lax.ppermute(value, "pipe", [(source, source + steps) for source in range(first, last)])


def dot_rows(left, right):
    return lax.dot_general(left, right, (((0,), (0,)), ((), ())), preferred_element_type=F32)


def dot_cols(left, right):
    return lax.dot_general(left, right, (((1,), (1,)), ((), ())), preferred_element_type=F32)


def dot(left, right):
    return lax.dot_general(left, right, (((1,), (0,)), ((), ())), preferred_element_type=F32)


def members(plane, routes, experts):
    tokens = routes.shape[1]
    height = -(-experts // 8) * 8
    expert = lax.broadcasted_iota(jnp.int32, (height, tokens), 0) ^ plane
    named = [routes[k : k + 1, :] == expert for k in range(routes.shape[0])]
    chosen = functools.reduce(jnp.logical_or, named)
    earlier = lax.broadcasted_iota(jnp.int32, (tokens, tokens), 0) < lax.broadcasted_iota(
        jnp.int32, (tokens, tokens), 1
    )
    rank = dot(chosen.astype(F32).astype(BF16), earlier.astype(F32).astype(BF16)).astype(jnp.int32)
    return chosen, rank, named


def slots_of(chosen, rank, d, slots):
    tokens = rank.shape[1]
    place = lax.broadcasted_iota(jnp.int32, (slots, tokens), 0)
    row = jnp.where(chosen[d : d + 1, :], rank[d : d + 1, :], -1)
    return place == row


def norm_factor(values_ref, chunk):
    tokens, width = values_ref.shape

    def add(i, total):
        part = values_ref[:, pl.ds(pl.multiple_of(i * chunk, chunk), chunk)].astype(F32)
        return total + jnp.sum(part * part, axis=1, keepdims=True)

    total = lax.fori_loop(0, width // chunk, add, jnp.zeros((tokens, 1), F32))
    return lax.rsqrt(total * (1.0 / width) + EPSILON)


def select_norm_kernel(experts, slots, plane_ref, routes_ref, values_ref, gain_ref, *out_refs):
    width = values_ref.shape[1]
    chunk = chunk_of(width)
    chosen, rank, _ = members(plane_ref[0], routes_ref[...], experts)
    picks = jnp.concatenate(
        [slots_of(chosen, rank, d, slots).astype(F32) for d in range(experts)], axis=0
    ).astype(BF16)
    inverse = norm_factor(values_ref, chunk)

    def step(i, carry):
        cols = pl.ds(pl.multiple_of(i * chunk, chunk), chunk)
        normed = values_ref[:, cols].astype(F32) * inverse
        rows = dot(picks, (normed * gain_ref[:, cols]).astype(BF16)).astype(BF16)
        for d in range(experts):
            out_refs[d][:, cols] = rows[d * slots : (d + 1) * slots]
        return carry

    lax.fori_loop(0, width // chunk, step, 0, unroll=True)


def select_both_kernel(
    experts, slots, plane_ref, routes_ref, gates_ref, values_ref, gain_ref, cot_ref, *out_refs
):
    width = values_ref.shape[1]
    chunk = chunk_of(width)
    chosen, rank, named = members(plane_ref[0], routes_ref[...], experts)
    gates = gates_ref[...].astype(F32)
    gate_of = sum(jnp.where(hit, gates[k : k + 1, :], 0.0) for k, hit in enumerate(named))
    hits = [slots_of(chosen, rank, d, slots) for d in range(experts)]
    picks = jnp.concatenate([hit.astype(F32) for hit in hits], axis=0).astype(BF16)
    gate_col = jnp.concatenate(
        [
            jnp.sum(jnp.where(hit, gate_of[d : d + 1, :], 0.0), axis=1, keepdims=True)
            for d, hit in enumerate(hits)
        ],
        axis=0,
    )
    inverse = norm_factor(values_ref, chunk)

    def step(i, carry):
        cols = pl.ds(pl.multiple_of(i * chunk, chunk), chunk)
        normed = values_ref[:, cols].astype(F32) * inverse
        rows = dot(picks, (normed * gain_ref[:, cols]).astype(BF16)).astype(BF16)
        scaled = (dot(picks, cot_ref[:, cols]) * gate_col).astype(BF16)
        for d in range(experts):
            out_refs[d][:, cols] = rows[d * slots : (d + 1) * slots]
            out_refs[experts + d][:, cols] = scaled[d * slots : (d + 1) * slots]
        return carry

    lax.fori_loop(0, width // chunk, step, 0, unroll=True)


def forward_kernel(rows_ref, gate_ref, up_ref, down_ref, out_ref):
    rows = rows_ref[...]
    pre_gate = dot(rows, gate_ref[...])
    pre_up = dot(rows, up_ref[...])
    act = (pre_gate * jax.nn.sigmoid(pre_gate) * pre_up).astype(BF16)
    width = out_ref.shape[1]
    chunk = chunk_of(width)

    def step(i, carry):
        cols = pl.ds(pl.multiple_of(i * chunk, chunk), chunk)
        out_ref[:, cols] = dot(act, down_ref[:, cols]).astype(BF16)
        return carry

    lax.fori_loop(0, width // chunk, step, 0, unroll=True)


def hidden_kernel(rows_ref, gate_ref, up_ref, act_ref, gate_factor_ref, up_factor_ref):
    rows = rows_ref[...]
    pre_gate = dot(rows, gate_ref[...])
    pre_up = dot(rows, up_ref[...])
    sigma = jax.nn.sigmoid(pre_gate)
    swish = pre_gate * sigma
    act_ref[...] = (swish * pre_up).astype(BF16)
    gate_factor_ref[...] = pre_up * sigma * (1.0 + pre_gate * (1.0 - sigma))
    up_factor_ref[...] = swish


def backward_kernel(
    rows_ref, cot_ref, act_ref, gate_factor_ref, up_factor_ref, gate_ref, up_ref, down_ref,
    out_ref, gate_grad_ref, up_grad_ref, gain_ref,
):
    width = gain_ref.shape[1]
    chunk = chunk_of(width)
    upstream = dot_cols(cot_ref[...], down_ref[...])
    gate_grad = (upstream * gate_factor_ref[...]).astype(BF16)
    up_grad = (upstream * up_factor_ref[...]).astype(BF16)
    gate_grad_ref[...] = gate_grad
    up_grad_ref[...] = up_grad
    term = jnp.sum(act_ref[...].astype(F32) * upstream, axis=1, keepdims=True)
    high = term.astype(BF16).astype(F32)
    lane = lax.broadcasted_iota(jnp.int32, (term.shape[0], LANES), 1)
    out_ref[:, width:] = jnp.where(lane < LANES // 2, high, term - high).astype(BF16)

    def step(i, carry):
        cols = pl.ds(pl.multiple_of(i * chunk, chunk), chunk)
        grads = dot_cols(gate_grad, gate_ref[cols, :]) + dot_cols(up_grad, up_ref[cols, :])
        out_ref[:, cols] = grads.astype(BF16)
        gain_ref[:, cols] = jnp.sum(grads * rows_ref[:, cols].astype(F32), axis=0, keepdims=True)
        return carry

    lax.fori_loop(0, width // chunk, step, 0, unroll=True)


def weight_kernel(
    own_ref, other_ref, cot_own, cot_other, act_own, act_other, gate_own, gate_other,
    up_own, up_other, grad_gate_ref, grad_up_ref, grad_down_ref,
):
    own, other = own_ref[...], other_ref[...]
    grad_gate_ref[...] = (dot_rows(own, gate_own[...]) + dot_rows(other, gate_other[...])).astype(
        BF16
    )
    grad_up_ref[...] = (dot_rows(own, up_own[...]) + dot_rows(other, up_other[...])).astype(BF16)
    grad_down_ref[...] = (
        dot_rows(act_own[...], cot_own[...]) + dot_rows(act_other[...], cot_other[...])
    ).astype(BF16)


def mixed_kernel(experts, slots, plane_ref, routes_ref, gates_ref, values_ref, *refs):
    block_refs, out_ref = refs[:experts], refs[experts]
    width = values_ref.shape[1]
    chunk = chunk_of(width)
    chosen, rank, named = members(plane_ref[0], routes_ref[...], experts)
    gates = gates_ref[...].astype(F32)
    gate_of = sum(jnp.where(hit, gates[k : k + 1, :], 0.0) for k, hit in enumerate(named))
    weights = [
        jnp.where(slots_of(chosen, rank, d, slots), gate_of[d : d + 1, :], 0.0).astype(BF16)
        for d in range(experts)
    ]

    def step(i, carry):
        cols = pl.ds(pl.multiple_of(i * chunk, chunk), chunk)
        total = sum(dot_rows(weights[d], block_refs[d][:, cols]) for d in range(experts))
        out_ref[:, cols] = (values_ref[:, cols].astype(F32) + total).astype(BF16)
        return carry

    lax.fori_loop(0, width // chunk, step, 0, unroll=True)


def input_grad_kernel(
    experts, slots, plane_ref, routes_ref, gates_ref, values_ref, cot_ref, gain_ref, *refs
):
    block_refs = refs[:experts]
    out_ref, gate_out_ref, scaled_ref = refs[experts:]
    tokens, width = values_ref.shape
    chunk = chunk_of(width)
    chosen, rank, named = members(plane_ref[0], routes_ref[...], experts)
    hits = [slots_of(chosen, rank, d, slots) for d in range(experts)]
    picks = [hit.astype(F32).astype(BF16) for hit in hits]
    inverse = norm_factor(values_ref, chunk)

    terms = []
    for named_k in named:
        total = jnp.zeros((LANES, tokens), F32)
        for d in range(experts):
            mine = jnp.where(named_k[d : d + 1, :], hits[d].astype(F32), 0.0).astype(BF16)
            total = total + dot_rows(block_refs[d][:, width:], mine)
        terms.append(total[0:1] + total[LANES // 2 : LANES // 2 + 1])
    gate_out_ref[...] = jnp.concatenate(terms, axis=0) / gates_ref[...].astype(F32)

    def first(i, carry):
        cols = pl.ds(pl.multiple_of(i * chunk, chunk), chunk)
        grads = sum(dot_rows(picks[d], block_refs[d][:, cols]) for d in range(experts))
        grads = grads * gain_ref[:, cols]
        scaled_ref[:, cols] = grads
        normed = values_ref[:, cols].astype(F32) * inverse
        return carry + jnp.sum(grads * normed, axis=1, keepdims=True)

    mean = lax.fori_loop(0, width // chunk, first, jnp.zeros((tokens, 1), F32)) * (1.0 / width)

    def second(i, carry):
        cols = pl.ds(pl.multiple_of(i * chunk, chunk), chunk)
        normed = values_ref[:, cols].astype(F32) * inverse
        out_ref[:, cols] = (
            cot_ref[:, cols].astype(F32) + inverse * (scaled_ref[:, cols] - normed * mean)
        ).astype(BF16)
        return carry

    lax.fori_loop(0, width // chunk, second, 0)


SMEM_SPEC = pl.BlockSpec(memory_space=pltpu.SMEM)
VMEM_SPEC = pl.BlockSpec(memory_space=pltpu.VMEM)


def call(body, out_shapes, args, name, scratch=(), scalars=0):
    return pl.pallas_call(
        body,
        out_shape=[jax.ShapeDtypeStruct(shape, dtype) for shape, dtype in out_shapes],
        in_specs=[SMEM_SPEC] * scalars + [VMEM_SPEC] * (len(args) - scalars),
        out_specs=[VMEM_SPEC] * len(out_shapes),
        scratch_shapes=list(scratch),
        cost_estimate=HINT,
        compiler_params=pltpu.CompilerParams(vmem_limit_bytes=48 << 20),
        name=name,
    )(*args)


def weight_grads(rows, cots, acts, gates, ups):
    count, width = rows[0].shape
    units = acts[0].shape[1]
    chunk = chunk_of(width)
    whole = pl.BlockSpec((count, units), lambda i: (0, 0))
    return pl.pallas_call(
        weight_kernel,
        grid=(width // chunk,),
        out_shape=[
            jax.ShapeDtypeStruct((width, units), BF16),
            jax.ShapeDtypeStruct((width, units), BF16),
            jax.ShapeDtypeStruct((units, width), BF16),
        ],
        in_specs=[pl.BlockSpec((count, chunk), lambda i: (0, i))] * 4 + [whole] * 6,
        out_specs=[
            pl.BlockSpec((chunk, units), lambda i: (i, 0)),
            pl.BlockSpec((chunk, units), lambda i: (i, 0)),
            pl.BlockSpec((units, chunk), lambda i: (0, i)),
        ],
        cost_estimate=HINT,
        compiler_params=pltpu.CompilerParams(vmem_limit_bytes=48 << 20),
        name="weight_grads",
    )(*rows, *cots, *acts, *gates, *ups)


def after(values, *earlier):
    return lax.optimization_barrier((tuple(values), tuple(earlier)))[0]


def join_kernel(pieces, *refs):
    in_refs, out_refs, sems = refs[: -len(pieces) - 1], refs[-len(pieces) - 1 : -1], refs[-1]
    copies, k = [], 0
    for out_ref, parts in zip(out_refs, pieces):
        row = 0
        for source, start, count in parts:
            copies.append(
                pltpu.make_async_copy(
                    in_refs[source].at[pl.ds(start, count)],
                    out_ref.at[pl.ds(row, count)],
                    sems.at[k],
                )
            )
            row += count
            k += 1
    for copy in copies:
        copy.start()
    for copy in copies:
        copy.wait()


def join(arrays, pieces, name):
    width = arrays[0].shape[1]
    pieces = tuple(tuple(parts) for parts in pieces)
    return pl.pallas_call(
        functools.partial(join_kernel, pieces),
        out_shape=[
            jax.ShapeDtypeStruct((sum(part[2] for part in parts), width), BF16)
            for parts in pieces
        ],
        in_specs=[pl.BlockSpec(memory_space=pl.ANY)] * len(arrays),
        out_specs=[VMEM_SPEC] * len(pieces),
        scratch_shapes=[pltpu.SemaphoreType.DMA((sum(len(parts) for parts in pieces),))],
        cost_estimate=HINT,
        compiler_params=pltpu.CompilerParams(vmem_limit_bytes=48 << 20),
        name=name,
    )(*arrays)


def part_of(own, partner, index, slots):
    rows = slice(index * slots, (index + 1) * slots)
    return own[rows].astype(F32) + partner[rows].astype(F32)


def on_device(
    fwd_input,
    fwd_routes,
    fwd_gates,
    bwd_input,
    bwd_routes,
    bwd_gates,
    out_grad,
    norm_gain,
    gate_weight,
    up_weight,
    down_weight,
):
    devices = lax.axis_size("expert")
    experts = devices // UNIT_SPLIT_COUNT
    tokens, width = fwd_input.shape[1:]
    picks = fwd_routes.shape[2]
    capacity = min(tokens, tokens * picks * 5 // (4 * experts))
    slots = -(-capacity // 8) * 8
    plane = (lax.axis_index("expert") // UNIT_SPLIT_COUNT).astype(jnp.int32).reshape(1)
    gate_matrix, up_matrix, down_matrix = gate_weight[0], up_weight[0], down_weight[0]
    units = gate_matrix.shape[1]
    fwd_ids, bwd_ids = fwd_routes[0].T, bwd_routes[0].T
    fwd_g, bwd_g = fwd_gates[0].T, bwd_gates[0].T

    fwd_blocks = call(
        functools.partial(select_norm_kernel, experts, slots),
        [((slots, width), BF16)] * experts,
        (plane, fwd_ids, fwd_input[0], norm_gain),
        "select_fwd",
        scalars=1,
    )
    both = call(
        functools.partial(select_both_kernel, experts, slots),
        [((slots, width), BF16)] * (2 * experts),
        (plane, bwd_ids, bwd_g, bwd_input[0], norm_gain, out_grad[0]),
        "select_bwd",
        scalars=1,
    )
    bwd_blocks, cot_blocks = both[:experts], both[experts:]
    rows = 2 * experts * slots

    def forward(rows_in, name):
        return call(
            forward_kernel,
            [((rows, width), BF16)],
            (rows_in, gate_matrix, up_matrix, down_matrix),
            name,
        )[0]

    def hidden(rows_in, name):
        return call(
            hidden_kernel,
            [((rows, units), BF16), ((rows, units), F32), ((rows, units), F32)],
            (rows_in, gate_matrix, up_matrix),
            name,
        )

    def backward(rows_in, cot_in, made, name):
        return call(
            backward_kernel,
            [((rows, width + LANES), BF16)] + [((rows, units), BF16)] * 2 + [((1, width), F32)],
            (rows_in, cot_in, *made, gate_matrix, up_matrix, down_matrix),
            name,
        )

    away = range(1, experts)
    far = (experts - 1) * slots
    half = experts * slots

    def over_z(blocks):
        return [swap(block, d * UNIT_SPLIT_COUNT) for d, block in zip(away, blocks)]

    laid_far = [(k, 0, slots) for k in range(experts - 1)]

    def laid_own(k, first):
        return [(first, 0, slots), (first + 1, 0, far), (first + 2, k * slots, slots), (first + 3, 0, far)]

    (near,) = join(
        [fwd_blocks[0], bwd_blocks[0], cot_blocks[0]],
        [[(k, 0, slots) for k in range(3)]],
        "near_blocks",
    )
    near_crossed, fwd_landed = swap(near, 2), over_z(fwd_blocks[1:])
    *bwd_send, near_crossed = after((*bwd_blocks[1:], near_crossed), *fwd_landed)
    (fwd_far,) = join([*fwd_landed, near_crossed], [laid_far], "far_fwd")
    *bwd_send, fwd_far = after((*bwd_send, fwd_far))
    bwd_landed, fwd_far_crossed = over_z(bwd_send), swap(fwd_far, 2)
    bwd_far, fwd_own = join(
        [*bwd_landed, fwd_blocks[0], fwd_far, near_crossed, fwd_far_crossed],
        [laid_far, laid_own(0, experts - 1)],
        "far_bwd_own_fwd",
    )
    *cot_send, bwd_far, fwd_own = after((*cot_blocks[1:], bwd_far, fwd_own))
    cot_landed, bwd_far_crossed, fwd_other = over_z(cot_send), swap(bwd_far, 2), swap(fwd_own, 1)
    out_own = forward(fwd_own, "forward_own")
    *cot_landed, bwd_far_crossed, fwd_other = after(
        (*cot_landed, bwd_far_crossed, fwd_other), out_own
    )
    cot_far, bwd_own = join(
        [*cot_landed, bwd_blocks[0], bwd_far, near_crossed, bwd_far_crossed],
        [laid_far, laid_own(1, experts - 1)],
        "far_cot_own_bwd",
    )
    cot_far, bwd_own, fwd_other = after((cot_far, bwd_own, fwd_other))
    cot_far_crossed, bwd_other = swap(cot_far, 2), swap(bwd_own, 1)
    out_other = forward(fwd_other, "forward_other")
    out_partner = swap(out_other, 1)
    made_own = hidden(bwd_own, "hidden_own")
    made_other = hidden(bwd_other, "hidden_other")
    cot_far_crossed, bwd_other, out_partner = after(
        (cot_far_crossed, bwd_other, out_partner), made_own[0], made_other[0]
    )
    (cot_own,) = join(
        [cot_blocks[0], cot_far, near_crossed, cot_far_crossed], [laid_own(2, 0)], "own_cot"
    )
    cot_own, out_partner = after((cot_own, out_partner))
    cot_other = swap(cot_own, 1)
    norm_own, dgate_own, dup_own, gain_own = backward(bwd_own, cot_own, made_own, "backward_own")
    norm_other, dgate_other, dup_other, gain_other = backward(
        bwd_other, cot_other, made_other, "backward_other"
    )
    norm_partner = swap(norm_other, 1)

    def crossing(own, partner, first, count):
        rows = slice(half + first * slots, half + (first + count) * slots)
        return (own[rows].astype(F32) + partner[rows].astype(F32)).astype(BF16)

    def send_home(own, partner, crossed, d):
        block = (part_of(own, partner, d, slots) + crossed.astype(F32)).astype(BF16)
        return swap(block, d * UNIT_SPLIT_COUNT) if d else block

    def go_back(own, partner, *held):
        middle = experts // 2
        low, high = crossing(own, partner, 0, middle), crossing(own, partner, middle, middle)
        low, high = after((low, high), *held)
        high_crossed = swap(high, 2)
        low_crossed = swap(low, 2)
        back = {}
        for d in range(experts)[::-1]:
            whole = high_crossed if d >= middle else low_crossed
            start = (d % middle) * slots
            back[d] = send_home(own, partner, whole[start : start + slots], d)
        return [back[d] for d in range(experts)], low_crossed

    out_back, out_low = go_back(out_own, out_partner)
    norm_back, norm_low = go_back(norm_own, norm_partner, out_low)
    out_back = after(out_back, norm_low)
    gain_sum = gain_own + gain_other
    gain_sum = gain_sum + swap(gain_sum, 1)
    (gain_sum,) = after((gain_sum,), norm_partner)
    gain_crossed = swap(gain_sum, 2)
    gain_sum, gain_crossed = after((gain_sum, gain_crossed), norm_low)
    gain_sum = gain_sum + gain_crossed
    gain_sum = sum([swap(gain_sum, d * UNIT_SPLIT_COUNT) for d in away], gain_sum)
    grad_gate, grad_up, grad_down = weight_grads(
        (bwd_own, bwd_other),
        (cot_own, cot_other),
        (made_own[0], made_other[0]),
        (dgate_own, dgate_other),
        (dup_own, dup_other),
    )
    gain_grad = gain_sum / norm_gain

    input_grad, gate_grad = call(
        functools.partial(input_grad_kernel, experts, slots),
        [((tokens, width), BF16), ((picks, tokens), F32)],
        (plane, bwd_ids, bwd_g, bwd_input[0], out_grad[0], norm_gain, *norm_back),
        "input_grad",
        scratch=[pltpu.VMEM((tokens, width), F32)],
        scalars=1,
    )
    mixed = call(
        functools.partial(mixed_kernel, experts, slots),
        [((tokens, width), BF16)],
        (plane, fwd_ids, fwd_g, fwd_input[0], *out_back),
        "mixed",
        scalars=1,
    )[0]
    act_next = along_pipe(mixed, 1)
    grad_prev = along_pipe(input_grad, -1)
    return (
        act_next[None],
        grad_prev[None],
        gate_grad.T[None],
        gain_grad,
        grad_gate[None],
        grad_up[None],
        grad_down[None],
    )


def solution(mesh):
    rows = P("pipe", "expert", None)
    columns = P("pipe", None, "expert")
    return jax.shard_map(
        on_device,
        mesh=mesh,
        in_specs=(rows,) * 7 + (P("pipe", None), columns, columns, rows),
        out_specs=(rows, rows, rows, P("pipe", None), columns, columns, rows),
        check_vma=False,
    )
```

```python
import functools

import jax
import jax.numpy as jnp
from jax import lax
from jax.experimental import pallas as pl
from jax.experimental.pallas import tpu as pltpu
from jax.sharding import PartitionSpec as P

UNIT_SPLIT_COUNT = 4
HINT = pl.CostEstimate(flops=10**11, transcendentals=0, bytes_accessed=1 << 20)
EPSILON = 1e-06
LANES = 128
BF16 = jnp.bfloat16
F32 = jnp.float32


def chunk_of(width):
    for size in (512, 256, 128):
        if width % size == 0:
            return size
    return width


def swap(value, mask):
    count = lax.axis_size("expert")
    return lax.ppermute(value, "expert", [(source, source ^ mask) for source in range(count)])


def along_pipe(value, steps):
    count = lax.axis_size("pipe")
    first, last = (max(0, -steps), min(count, count - steps))
    return lax.ppermute(value, "pipe", [(source, source + steps) for source in range(first, last)])


def dot_rows(left, right):
    return lax.dot_general(left, right, (((0,), (0,)), ((), ())), preferred_element_type=F32)


def dot_cols(left, right):
    return lax.dot_general(left, right, (((1,), (1,)), ((), ())), preferred_element_type=F32)


def dot(left, right):
    return lax.dot_general(left, right, (((1,), (0,)), ((), ())), preferred_element_type=F32)


def members(plane, routes, experts):
    tokens = routes.shape[1]
    height = -(-experts // 8) * 8
    expert = lax.broadcasted_iota(jnp.int32, (height, tokens), 0) ^ plane
    named = [routes[k : k + 1, :] == expert for k in range(routes.shape[0])]
    chosen = functools.reduce(jnp.logical_or, named)
    earlier = lax.broadcasted_iota(jnp.int32, (tokens, tokens), 0) < lax.broadcasted_iota(
        jnp.int32, (tokens, tokens), 1
    )
    rank = dot(chosen.astype(F32).astype(BF16), earlier.astype(F32).astype(BF16)).astype(jnp.int32)
    return chosen, rank, named


def slots_of(chosen, rank, d, slots):
    tokens = rank.shape[1]
    place = lax.broadcasted_iota(jnp.int32, (slots, tokens), 0)
    row = jnp.where(chosen[d : d + 1, :], rank[d : d + 1, :], -1)
    return place == row


def norm_factor(values_ref, chunk):
    tokens, width = values_ref.shape

    def add(i, total):
        part = values_ref[:, pl.ds(pl.multiple_of(i * chunk, chunk), chunk)].astype(F32)
        return total + jnp.sum(part * part, axis=1, keepdims=True)

    total = lax.fori_loop(0, width // chunk, add, jnp.zeros((tokens, 1), F32))
    return lax.rsqrt(total * (1.0 / width) + EPSILON)


def select_norm_kernel(experts, slots, plane_ref, routes_ref, values_ref, gain_ref, *out_refs):
    width = values_ref.shape[1]
    chunk = chunk_of(width)
    chosen, rank, _ = members(plane_ref[0], routes_ref[...], experts)
    picks = jnp.concatenate(
        [slots_of(chosen, rank, d, slots).astype(F32) for d in range(experts)], axis=0
    ).astype(BF16)
    inverse = norm_factor(values_ref, chunk)

    def step(i, carry):
        cols = pl.ds(pl.multiple_of(i * chunk, chunk), chunk)
        normed = values_ref[:, cols].astype(F32) * inverse
        rows = dot(picks, (normed * gain_ref[:, cols]).astype(BF16)).astype(BF16)
        for d in range(experts):
            out_refs[d][:, cols] = rows[d * slots : (d + 1) * slots]
        return carry

    lax.fori_loop(0, width // chunk, step, 0, unroll=True)


def select_both_kernel(
    experts, slots, plane_ref, routes_ref, gates_ref, values_ref, gain_ref, cot_ref, *out_refs
):
    width = values_ref.shape[1]
    chunk = chunk_of(width)
    chosen, rank, named = members(plane_ref[0], routes_ref[...], experts)
    gates = gates_ref[...].astype(F32)
    gate_of = sum(jnp.where(hit, gates[k : k + 1, :], 0.0) for k, hit in enumerate(named))
    hits = [slots_of(chosen, rank, d, slots) for d in range(experts)]
    picks = jnp.concatenate([hit.astype(F32) for hit in hits], axis=0).astype(BF16)
    gate_col = jnp.concatenate(
        [
            jnp.sum(jnp.where(hit, gate_of[d : d + 1, :], 0.0), axis=1, keepdims=True)
            for d, hit in enumerate(hits)
        ],
        axis=0,
    )
    inverse = norm_factor(values_ref, chunk)

    def step(i, carry):
        cols = pl.ds(pl.multiple_of(i * chunk, chunk), chunk)
        normed = values_ref[:, cols].astype(F32) * inverse
        rows = dot(picks, (normed * gain_ref[:, cols]).astype(BF16)).astype(BF16)
        scaled = (dot(picks, cot_ref[:, cols]) * gate_col).astype(BF16)
        for d in range(experts):
            out_refs[d][:, cols] = rows[d * slots : (d + 1) * slots]
            out_refs[experts + d][:, cols] = scaled[d * slots : (d + 1) * slots]
        return carry

    lax.fori_loop(0, width // chunk, step, 0, unroll=True)


def forward_kernel(rows_ref, gate_ref, up_ref, down_ref, out_ref):
    rows = rows_ref[...]
    pre_gate = dot(rows, gate_ref[...])
    pre_up = dot(rows, up_ref[...])
    act = (pre_gate * jax.nn.sigmoid(pre_gate) * pre_up).astype(BF16)
    width = out_ref.shape[1]
    chunk = chunk_of(width)

    def step(i, carry):
        cols = pl.ds(pl.multiple_of(i * chunk, chunk), chunk)
        out_ref[:, cols] = dot(act, down_ref[:, cols]).astype(BF16)
        return carry

    lax.fori_loop(0, width // chunk, step, 0, unroll=True)


def hidden_kernel(rows_ref, gate_ref, up_ref, act_ref, gate_factor_ref, up_factor_ref):
    rows = rows_ref[...]
    pre_gate = dot(rows, gate_ref[...])
    pre_up = dot(rows, up_ref[...])
    sigma = jax.nn.sigmoid(pre_gate)
    swish = pre_gate * sigma
    act_ref[...] = (swish * pre_up).astype(BF16)
    gate_factor_ref[...] = pre_up * sigma * (1.0 + pre_gate * (1.0 - sigma))
    up_factor_ref[...] = swish


def backward_kernel(
    rows_ref, cot_ref, act_ref, gate_factor_ref, up_factor_ref, gate_ref, up_ref, down_ref,
    out_ref, gate_grad_ref, up_grad_ref, gain_ref,
):
    width = gain_ref.shape[1]
    chunk = chunk_of(width)
    upstream = dot_cols(cot_ref[...], down_ref[...])
    gate_grad = (upstream * gate_factor_ref[...]).astype(BF16)
    up_grad = (upstream * up_factor_ref[...]).astype(BF16)
    gate_grad_ref[...] = gate_grad
    up_grad_ref[...] = up_grad
    term = jnp.sum(act_ref[...].astype(F32) * upstream, axis=1, keepdims=True)
    high = term.astype(BF16).astype(F32)
    lane = lax.broadcasted_iota(jnp.int32, (term.shape[0], LANES), 1)
    out_ref[:, width:] = jnp.where(lane < LANES // 2, high, term - high).astype(BF16)

    def step(i, carry):
        cols = pl.ds(pl.multiple_of(i * chunk, chunk), chunk)
        grads = dot_cols(gate_grad, gate_ref[cols, :]) + dot_cols(up_grad, up_ref[cols, :])
        out_ref[:, cols] = grads.astype(BF16)
        gain_ref[:, cols] = jnp.sum(grads * rows_ref[:, cols].astype(F32), axis=0, keepdims=True)
        return carry

    lax.fori_loop(0, width // chunk, step, 0, unroll=True)


def weight_kernel(
    own_ref, other_ref, cot_own, cot_other, act_own, act_other, gate_own, gate_other,
    up_own, up_other, grad_gate_ref, grad_up_ref, grad_down_ref,
):
    own, other = own_ref[...], other_ref[...]
    grad_gate_ref[...] = (dot_rows(own, gate_own[...]) + dot_rows(other, gate_other[...])).astype(
        BF16
    )
    grad_up_ref[...] = (dot_rows(own, up_own[...]) + dot_rows(other, up_other[...])).astype(BF16)
    grad_down_ref[...] = (
        dot_rows(act_own[...], cot_own[...]) + dot_rows(act_other[...], cot_other[...])
    ).astype(BF16)


def add_kernel(first, slots, own_ref, partner_ref, crossed_ref, *out_refs):
    for i, out_ref in enumerate(out_refs):
        rows, landed = pl.ds((first + i) * slots, slots), pl.ds(i * slots, slots)
        total = own_ref[rows, :].astype(F32) + partner_ref[rows, :].astype(F32)
        out_ref[...] = (total + crossed_ref[landed, :].astype(F32)).astype(BF16)


def mixed_kernel(experts, slots, plane_ref, routes_ref, gates_ref, values_ref, *refs):
    block_refs, out_ref = refs[:experts], refs[experts]
    width = values_ref.shape[1]
    chunk = chunk_of(width)
    chosen, rank, named = members(plane_ref[0], routes_ref[...], experts)
    gates = gates_ref[...].astype(F32)
    gate_of = sum(jnp.where(hit, gates[k : k + 1, :], 0.0) for k, hit in enumerate(named))
    weights = [
        jnp.where(slots_of(chosen, rank, d, slots), gate_of[d : d + 1, :], 0.0).astype(BF16)
        for d in range(experts)
    ]

    def step(i, carry):
        cols = pl.ds(pl.multiple_of(i * chunk, chunk), chunk)
        total = sum(dot_rows(weights[d], block_refs[d][:, cols]) for d in range(experts))
        out_ref[:, cols] = (values_ref[:, cols].astype(F32) + total).astype(BF16)
        return carry

    lax.fori_loop(0, width // chunk, step, 0, unroll=True)


def input_grad_kernel(
    experts, slots, plane_ref, routes_ref, gates_ref, values_ref, cot_ref, gain_ref, *refs
):
    block_refs = refs[:experts]
    out_ref, gate_out_ref, scaled_ref = refs[experts:]
    tokens, width = values_ref.shape
    chunk = chunk_of(width)
    chosen, rank, named = members(plane_ref[0], routes_ref[...], experts)
    hits = [slots_of(chosen, rank, d, slots) for d in range(experts)]
    picks = [hit.astype(F32).astype(BF16) for hit in hits]
    inverse = norm_factor(values_ref, chunk)

    terms = []
    for named_k in named:
        total = jnp.zeros((LANES, tokens), F32)
        for d in range(experts):
            mine = jnp.where(named_k[d : d + 1, :], hits[d].astype(F32), 0.0).astype(BF16)
            total = total + dot_rows(block_refs[d][:, width:], mine)
        terms.append(total[0:1] + total[LANES // 2 : LANES // 2 + 1])
    gate_out_ref[...] = jnp.concatenate(terms, axis=0) / gates_ref[...].astype(F32)

    def first(i, carry):
        cols = pl.ds(pl.multiple_of(i * chunk, chunk), chunk)
        grads = sum(dot_rows(picks[d], block_refs[d][:, cols]) for d in range(experts))
        grads = grads * gain_ref[:, cols]
        scaled_ref[:, cols] = grads
        normed = values_ref[:, cols].astype(F32) * inverse
        return carry + jnp.sum(grads * normed, axis=1, keepdims=True)

    mean = lax.fori_loop(0, width // chunk, first, jnp.zeros((tokens, 1), F32)) * (1.0 / width)

    def second(i, carry):
        cols = pl.ds(pl.multiple_of(i * chunk, chunk), chunk)
        normed = values_ref[:, cols].astype(F32) * inverse
        out_ref[:, cols] = (
            cot_ref[:, cols].astype(F32) + inverse * (scaled_ref[:, cols] - normed * mean)
        ).astype(BF16)
        return carry

    lax.fori_loop(0, width // chunk, second, 0)


SMEM_SPEC = pl.BlockSpec(memory_space=pltpu.SMEM)
VMEM_SPEC = pl.BlockSpec(memory_space=pltpu.VMEM)


def call(body, out_shapes, args, name, scratch=(), scalars=0, hint=HINT):
    return pl.pallas_call(
        body,
        out_shape=[jax.ShapeDtypeStruct(shape, dtype) for shape, dtype in out_shapes],
        in_specs=[SMEM_SPEC] * scalars + [VMEM_SPEC] * (len(args) - scalars),
        out_specs=[VMEM_SPEC] * len(out_shapes),
        scratch_shapes=list(scratch),
        cost_estimate=hint,
        compiler_params=pltpu.CompilerParams(vmem_limit_bytes=12 << 20),
        name=name,
    )(*args)


def weight_grads(rows, cots, acts, gates, ups):
    count, width = rows[0].shape
    units = acts[0].shape[1]
    chunk = chunk_of(width)
    whole = pl.BlockSpec((count, units), lambda i: (0, 0))
    return pl.pallas_call(
        weight_kernel,
        grid=(width // chunk,),
        out_shape=[
            jax.ShapeDtypeStruct((width, units), BF16),
            jax.ShapeDtypeStruct((width, units), BF16),
            jax.ShapeDtypeStruct((units, width), BF16),
        ],
        in_specs=[pl.BlockSpec((count, chunk), lambda i: (0, i))] * 4 + [whole] * 6,
        out_specs=[
            pl.BlockSpec((chunk, units), lambda i: (i, 0)),
            pl.BlockSpec((chunk, units), lambda i: (i, 0)),
            pl.BlockSpec((units, chunk), lambda i: (0, i)),
        ],
        cost_estimate=HINT,
        compiler_params=pltpu.CompilerParams(vmem_limit_bytes=20 << 20),
        name="weight_grads",
    )(*rows, *cots, *acts, *gates, *ups)


def after(values, *earlier):
    return lax.optimization_barrier((tuple(values), tuple(earlier)))[0]


def join_kernel(pieces, *refs):
    in_refs, out_refs, sems = refs[: -len(pieces) - 1], refs[-len(pieces) - 1 : -1], refs[-1]
    copies, k = [], 0
    for out_ref, parts in zip(out_refs, pieces):
        row = 0
        for source, start, count in parts:
            copies.append(
                pltpu.make_async_copy(
                    in_refs[source].at[pl.ds(start, count)],
                    out_ref.at[pl.ds(row, count)],
                    sems.at[k],
                )
            )
            row += count
            k += 1
    for copy in copies:
        copy.start()
    for copy in copies:
        copy.wait()


def join(arrays, pieces, name):
    width = arrays[0].shape[1]
    pieces = tuple(tuple(parts) for parts in pieces)
    return pl.pallas_call(
        functools.partial(join_kernel, pieces),
        out_shape=[
            jax.ShapeDtypeStruct((sum(part[2] for part in parts), width), BF16)
            for parts in pieces
        ],
        in_specs=[pl.BlockSpec(memory_space=pl.ANY)] * len(arrays),
        out_specs=[VMEM_SPEC] * len(pieces),
        scratch_shapes=[pltpu.SemaphoreType.DMA((sum(len(parts) for parts in pieces),))],
        cost_estimate=HINT,
        compiler_params=pltpu.CompilerParams(vmem_limit_bytes=4 << 20),
        name=name,
    )(*arrays)


def part_of(own, partner, index, slots):
    rows = slice(index * slots, (index + 1) * slots)
    return own[rows].astype(F32) + partner[rows].astype(F32)


def on_device(
    fwd_input,
    fwd_routes,
    fwd_gates,
    bwd_input,
    bwd_routes,
    bwd_gates,
    out_grad,
    norm_gain,
    gate_weight,
    up_weight,
    down_weight,
):
    devices = lax.axis_size("expert")
    experts = devices // UNIT_SPLIT_COUNT
    tokens, width = fwd_input.shape[1:]
    picks = fwd_routes.shape[2]
    capacity = min(tokens, tokens * picks * 5 // (4 * experts))
    slots = -(-capacity // 8) * 8
    plane = (lax.axis_index("expert") // UNIT_SPLIT_COUNT).astype(jnp.int32).reshape(1)
    gate_matrix, up_matrix, down_matrix = gate_weight[0], up_weight[0], down_weight[0]
    units = gate_matrix.shape[1]
    fwd_ids, bwd_ids = fwd_routes[0].T, bwd_routes[0].T
    fwd_g, bwd_g = fwd_gates[0].T, bwd_gates[0].T

    fwd_blocks = call(
        functools.partial(select_norm_kernel, experts, slots),
        [((slots, width), BF16)] * experts,
        (plane, fwd_ids, fwd_input[0], norm_gain),
        "select_fwd",
        scalars=1,
    )
    both = call(
        functools.partial(select_both_kernel, experts, slots),
        [((slots, width), BF16)] * (2 * experts),
        (plane, bwd_ids, bwd_g, bwd_input[0], norm_gain, out_grad[0]),
        "select_bwd",
        scalars=1,
    )
    bwd_blocks, cot_blocks = both[:experts], both[experts:]
    rows = 2 * experts * slots

    def forward(rows_in, name):
        return call(
            forward_kernel,
            [((rows, width), BF16)],
            (rows_in, gate_matrix, up_matrix, down_matrix),
            name,
        )[0]

    def hidden(rows_in, name):
        return call(
            hidden_kernel,
            [((rows, units), BF16), ((rows, units), F32), ((rows, units), F32)],
            (rows_in, gate_matrix, up_matrix),
            name,
        )

    def backward(rows_in, cot_in, made, name):
        return call(
            backward_kernel,
            [((rows, width + LANES), BF16)] + [((rows, units), BF16)] * 2 + [((1, width), F32)],
            (rows_in, cot_in, *made, gate_matrix, up_matrix, down_matrix),
            name,
        )

    away = range(1, experts)
    far = (experts - 1) * slots
    half = experts * slots

    def over_z(blocks):
        return [swap(block, d * UNIT_SPLIT_COUNT) for d, block in zip(away, blocks)]

    laid_far = [(k, 0, slots) for k in range(experts - 1)]

    def laid_own(k, first):
        return [(first, 0, slots), (first + 1, 0, far), (first + 2, k * slots, slots), (first + 3, 0, far)]

    (near,) = join(
        [fwd_blocks[0], bwd_blocks[0], cot_blocks[0]],
        [[(k, 0, slots) for k in range(3)]],
        "near_blocks",
    )
    near_crossed, fwd_landed = swap(near, 2), over_z(fwd_blocks[1:])
    *bwd_send, near_crossed = after((*bwd_blocks[1:], near_crossed), *fwd_landed)
    (fwd_far,) = join([*fwd_landed, near_crossed], [laid_far], "far_fwd")
    *bwd_send, fwd_far = after((*bwd_send, fwd_far))
    bwd_landed, fwd_far_crossed = over_z(bwd_send), swap(fwd_far, 2)
    bwd_far, fwd_own = join(
        [*bwd_landed, fwd_blocks[0], fwd_far, near_crossed, fwd_far_crossed],
        [laid_far, laid_own(0, experts - 1)],
        "far_bwd_own_fwd",
    )
    *cot_send, bwd_far, fwd_own = after((*cot_blocks[1:], bwd_far, fwd_own))
    cot_landed, bwd_far_crossed, fwd_other = over_z(cot_send), swap(bwd_far, 2), swap(fwd_own, 1)
    out_own = forward(fwd_own, "forward_own")
    *cot_landed, bwd_far_crossed, fwd_other = after(
        (*cot_landed, bwd_far_crossed, fwd_other), out_own
    )
    cot_far, bwd_own = join(
        [*cot_landed, bwd_blocks[0], bwd_far, near_crossed, bwd_far_crossed],
        [laid_far, laid_own(1, experts - 1)],
        "far_cot_own_bwd",
    )
    cot_far, bwd_own, fwd_other = after((cot_far, bwd_own, fwd_other))
    cot_far_crossed, bwd_other = swap(cot_far, 2), swap(bwd_own, 1)
    out_other = forward(fwd_other, "forward_other")
    out_partner = swap(out_other, 1)
    made_own = hidden(bwd_own, "hidden_own")
    made_other = hidden(bwd_other, "hidden_other")
    cot_far_crossed, bwd_other, out_partner = after(
        (cot_far_crossed, bwd_other, out_partner), made_own[0], made_other[0]
    )
    (cot_own,) = join(
        [cot_blocks[0], cot_far, near_crossed, cot_far_crossed], [laid_own(2, 0)], "own_cot"
    )
    cot_own, out_partner = after((cot_own, out_partner))
    cot_other = swap(cot_own, 1)
    middle = experts // 2

    def crossing(own, partner, first, count):
        rows = slice(half + first * slots, half + (first + count) * slots)
        return (own[rows].astype(F32) + partner[rows].astype(F32)).astype(BF16)

    def home(own, partner, crossed, first):
        sums = call(
            functools.partial(add_kernel, first, slots),
            [((slots, own.shape[1]), BF16)] * middle,
            (own, partner, crossed),
            "add_columns",
            hint=None,
        )
        back = {}
        for i in range(middle)[::-1]:
            d = first + i
            back[i] = swap(sums[i], d * UNIT_SPLIT_COUNT) if d else sums[i]
        return [back[i] for i in range(middle)]

    out_high = swap(crossing(out_own, out_partner, middle, middle), 2)
    out_low = swap(crossing(out_own, out_partner, 0, middle), 2)
    norm_other, dgate_other, dup_other, gain_other = backward(
        bwd_other, cot_other, made_other, "backward_other"
    )
    norm_partner = swap(norm_other, 1)
    norm_own, dgate_own, dup_own, gain_own = backward(bwd_own, cot_own, made_own, "backward_own")
    (out_high,) = after((out_high,), norm_own)
    out_far = home(out_own, out_partner, out_high, middle)
    norm_high = swap(crossing(norm_own, norm_partner, middle, middle), 2)
    norm_low = swap(crossing(norm_own, norm_partner, 0, middle), 2)
    (dgate_own,) = after((dgate_own,), out_high, norm_partner)
    grad_gate, grad_up, grad_down = weight_grads(
        (bwd_own, bwd_other),
        (cot_own, cot_other),
        (made_own[0], made_other[0]),
        (dgate_own, dgate_other),
        (dup_own, dup_other),
    )
    held_high, out_low = after((norm_high, out_low), grad_gate)
    norm_far = home(norm_own, norm_partner, held_high, middle)
    out_near = home(out_own, out_partner, out_low, 0)
    out_back = after(out_near + out_far, held_high)
    mixed = call(
        functools.partial(mixed_kernel, experts, slots),
        [((tokens, width), BF16)],
        (plane, fwd_ids, fwd_g, fwd_input[0], *out_back),
        "mixed",
        scalars=1,
    )[0]
    low_own, low_partner, held_low = after((norm_own, norm_partner, norm_low), mixed)
    norm_near = home(low_own, low_partner, held_low, 0)
    norm_back = norm_near + norm_far
    gain_sum = gain_own + gain_other
    gain_sum = gain_sum + swap(gain_sum, 1)
    (gain_sum,) = after((gain_sum,), norm_partner)
    gain_crossed = swap(gain_sum, 2)
    gain_sum, gain_crossed = after((gain_sum, gain_crossed), mixed)
    gain_sum = gain_sum + gain_crossed
    gain_sum = sum([swap(gain_sum, d * UNIT_SPLIT_COUNT) for d in away], gain_sum)
    gain_grad = gain_sum / norm_gain

    input_grad, gate_grad = call(
        functools.partial(input_grad_kernel, experts, slots),
        [((tokens, width), BF16), ((picks, tokens), F32)],
        (plane, bwd_ids, bwd_g, bwd_input[0], out_grad[0], norm_gain, *norm_back),
        "input_grad",
        scratch=[pltpu.VMEM((tokens, width), F32)],
        scalars=1,
    )
    act_next = along_pipe(mixed, 1)
    grad_prev = along_pipe(input_grad, -1)
    return (
        act_next[None],
        grad_prev[None],
        gate_grad.T[None],
        gain_grad,
        grad_gate[None],
        grad_up[None],
        grad_down[None],
    )


def solution(mesh):
    rows = P("pipe", "expert", None)
    columns = P("pipe", None, "expert")
    return jax.shard_map(
        on_device,
        mesh=mesh,
        in_specs=(rows,) * 7 + (P("pipe", None), columns, columns, rows),
        out_specs=(rows, rows, rows, P("pipe", None), columns, columns, rows),
        check_vma=False,
    )
```

```python
import functools

import jax
import jax.numpy as jnp
from jax import lax
from jax.experimental import pallas as pl
from jax.experimental.pallas import tpu as pltpu
from jax.sharding import PartitionSpec as P

UNIT_SPLIT_COUNT = 4
HINT = pl.CostEstimate(flops=10**11, transcendentals=0, bytes_accessed=1 << 20)
EPSILON = 1e-06
LANES = 128
BF16 = jnp.bfloat16
F32 = jnp.float32


def chunk_of(width):
    for size in (512, 256, 128):
        if width % size == 0:
            return size
    return width


def swap(value, mask):
    count = lax.axis_size("expert")
    return lax.ppermute(value, "expert", [(source, source ^ mask) for source in range(count)])


def along_pipe(value, steps):
    count = lax.axis_size("pipe")
    first, last = (max(0, -steps), min(count, count - steps))
    return lax.ppermute(value, "pipe", [(source, source + steps) for source in range(first, last)])


def dot_rows(left, right):
    return lax.dot_general(left, right, (((0,), (0,)), ((), ())), preferred_element_type=F32)


def dot_cols(left, right):
    return lax.dot_general(left, right, (((1,), (1,)), ((), ())), preferred_element_type=F32)


def dot(left, right):
    return lax.dot_general(left, right, (((1,), (0,)), ((), ())), preferred_element_type=F32)


def members(plane, routes, experts):
    tokens = routes.shape[1]
    height = -(-experts // 8) * 8
    expert = lax.broadcasted_iota(jnp.int32, (height, tokens), 0) ^ plane
    named = [routes[k : k + 1, :] == expert for k in range(routes.shape[0])]
    chosen = functools.reduce(jnp.logical_or, named)
    earlier = lax.broadcasted_iota(jnp.int32, (tokens, tokens), 0) < lax.broadcasted_iota(
        jnp.int32, (tokens, tokens), 1
    )
    rank = dot(chosen.astype(F32).astype(BF16), earlier.astype(F32).astype(BF16)).astype(jnp.int32)
    return chosen, rank, named


def slots_of(chosen, rank, d, slots):
    tokens = rank.shape[1]
    place = lax.broadcasted_iota(jnp.int32, (slots, tokens), 0)
    row = jnp.where(chosen[d : d + 1, :], rank[d : d + 1, :], -1)
    return place == row


def norm_factor(values_ref, chunk):
    tokens, width = values_ref.shape

    def add(i, total):
        part = values_ref[:, pl.ds(pl.multiple_of(i * chunk, chunk), chunk)].astype(F32)
        return total + jnp.sum(part * part, axis=1, keepdims=True)

    total = lax.fori_loop(0, width // chunk, add, jnp.zeros((tokens, 1), F32), unroll=True)
    return lax.rsqrt(total * (1.0 / width) + EPSILON)


def select_norm_kernel(experts, slots, plane_ref, routes_ref, values_ref, gain_ref, *out_refs):
    width = values_ref.shape[1]
    chunk = chunk_of(width)
    chosen, rank, _ = members(plane_ref[0], routes_ref[...], experts)
    picks = jnp.concatenate(
        [slots_of(chosen, rank, d, slots).astype(F32) for d in range(experts)], axis=0
    ).astype(BF16)
    inverse = norm_factor(values_ref, chunk)

    def step(i, carry):
        cols = pl.ds(pl.multiple_of(i * chunk, chunk), chunk)
        normed = values_ref[:, cols].astype(F32) * inverse
        rows = dot(picks, (normed * gain_ref[:, cols]).astype(BF16)).astype(BF16)
        for d in range(experts):
            out_refs[d][:, cols] = rows[d * slots : (d + 1) * slots]
        return carry

    lax.fori_loop(0, width // chunk, step, 0, unroll=True)


def select_both_kernel(
    experts, slots, plane_ref, routes_ref, gates_ref, values_ref, gain_ref, cot_ref, *out_refs
):
    width = values_ref.shape[1]
    chunk = chunk_of(width)
    chosen, rank, named = members(plane_ref[0], routes_ref[...], experts)
    gates = gates_ref[...].astype(F32)
    gate_of = sum(jnp.where(hit, gates[k : k + 1, :], 0.0) for k, hit in enumerate(named))
    hits = [slots_of(chosen, rank, d, slots) for d in range(experts)]
    picks = jnp.concatenate([hit.astype(F32) for hit in hits], axis=0).astype(BF16)
    gate_col = jnp.concatenate(
        [
            jnp.sum(jnp.where(hit, gate_of[d : d + 1, :], 0.0), axis=1, keepdims=True)
            for d, hit in enumerate(hits)
        ],
        axis=0,
    )
    inverse = norm_factor(values_ref, chunk)

    def step(i, carry):
        cols = pl.ds(pl.multiple_of(i * chunk, chunk), chunk)
        normed = values_ref[:, cols].astype(F32) * inverse
        rows = dot(picks, (normed * gain_ref[:, cols]).astype(BF16)).astype(BF16)
        scaled = (dot(picks, cot_ref[:, cols]) * gate_col).astype(BF16)
        for d in range(experts):
            out_refs[d][:, cols] = rows[d * slots : (d + 1) * slots]
            out_refs[experts + d][:, cols] = scaled[d * slots : (d + 1) * slots]
        return carry

    lax.fori_loop(0, width // chunk, step, 0, unroll=True)


def forward_kernel(rows_ref, gate_ref, up_ref, down_ref, out_ref):
    rows = rows_ref[...]
    pre_gate = dot(rows, gate_ref[...])
    pre_up = dot(rows, up_ref[...])
    act = (pre_gate * jax.nn.sigmoid(pre_gate) * pre_up).astype(BF16)
    width = out_ref.shape[1]
    chunk = chunk_of(width)

    def step(i, carry):
        cols = pl.ds(pl.multiple_of(i * chunk, chunk), chunk)
        out_ref[:, cols] = dot(act, down_ref[:, cols]).astype(BF16)
        return carry

    lax.fori_loop(0, width // chunk, step, 0, unroll=True)


def hidden_kernel(rows_ref, gate_ref, up_ref, act_ref, gate_factor_ref, up_factor_ref):
    rows = rows_ref[...]
    pre_gate = dot(rows, gate_ref[...])
    pre_up = dot(rows, up_ref[...])
    sigma = jax.nn.sigmoid(pre_gate)
    swish = pre_gate * sigma
    act_ref[...] = (swish * pre_up).astype(BF16)
    gate_factor_ref[...] = pre_up * sigma * (1.0 + pre_gate * (1.0 - sigma))
    up_factor_ref[...] = swish


def backward_kernel(
    rows_ref, cot_ref, act_ref, gate_factor_ref, up_factor_ref, gate_ref, up_ref, down_ref,
    out_ref, gate_grad_ref, up_grad_ref, gain_ref,
):
    width = gain_ref.shape[1]
    chunk = chunk_of(width)
    upstream = dot_cols(cot_ref[...], down_ref[...])
    gate_grad = (upstream * gate_factor_ref[...]).astype(BF16)
    up_grad = (upstream * up_factor_ref[...]).astype(BF16)
    gate_grad_ref[...] = gate_grad
    up_grad_ref[...] = up_grad
    term = jnp.sum(act_ref[...].astype(F32) * upstream, axis=1, keepdims=True)
    high = term.astype(BF16).astype(F32)
    lane = lax.broadcasted_iota(jnp.int32, (term.shape[0], LANES), 1)
    out_ref[:, width:] = jnp.where(lane < LANES // 2, high, term - high).astype(BF16)

    def step(i, carry):
        cols = pl.ds(pl.multiple_of(i * chunk, chunk), chunk)
        grads = dot_cols(gate_grad, gate_ref[cols, :]) + dot_cols(up_grad, up_ref[cols, :])
        out_ref[:, cols] = grads.astype(BF16)
        gain_ref[:, cols] = jnp.sum(grads * rows_ref[:, cols].astype(F32), axis=0, keepdims=True)
        return carry

    lax.fori_loop(0, width // chunk, step, 0, unroll=True)


def weight_kernel(
    own_ref, other_ref, cot_own, cot_other, act_own, act_other, gate_own, gate_other,
    up_own, up_other, grad_gate_ref, grad_up_ref, grad_down_ref,
):
    own, other = own_ref[...], other_ref[...]
    grad_gate_ref[...] = (dot_rows(own, gate_own[...]) + dot_rows(other, gate_other[...])).astype(
        BF16
    )
    grad_up_ref[...] = (dot_rows(own, up_own[...]) + dot_rows(other, up_other[...])).astype(BF16)
    grad_down_ref[...] = (
        dot_rows(act_own[...], cot_own[...]) + dot_rows(act_other[...], cot_other[...])
    ).astype(BF16)


def add_kernel(first, slots, own_ref, partner_ref, crossed_ref, *out_refs):
    for i, out_ref in enumerate(out_refs):
        rows, landed = pl.ds((first + i) * slots, slots), pl.ds(i * slots, slots)
        total = own_ref[rows, :].astype(F32) + partner_ref[rows, :].astype(F32)
        out_ref[...] = (total + crossed_ref[landed, :].astype(F32)).astype(BF16)


def mixed_kernel(experts, slots, plane_ref, routes_ref, gates_ref, values_ref, *refs):
    block_refs, out_ref = refs[:experts], refs[experts]
    width = values_ref.shape[1]
    chunk = chunk_of(width)
    chosen, rank, named = members(plane_ref[0], routes_ref[...], experts)
    gates = gates_ref[...].astype(F32)
    gate_of = sum(jnp.where(hit, gates[k : k + 1, :], 0.0) for k, hit in enumerate(named))
    weights = [
        jnp.where(slots_of(chosen, rank, d, slots), gate_of[d : d + 1, :], 0.0).astype(BF16)
        for d in range(experts)
    ]

    def step(i, carry):
        cols = pl.ds(pl.multiple_of(i * chunk, chunk), chunk)
        total = sum(dot_rows(weights[d], block_refs[d][:, cols]) for d in range(experts))
        out_ref[:, cols] = (values_ref[:, cols].astype(F32) + total).astype(BF16)
        return carry

    lax.fori_loop(0, width // chunk, step, 0, unroll=True)


def input_grad_kernel(
    experts, slots, plane_ref, routes_ref, gates_ref, values_ref, cot_ref, gain_ref, *refs
):
    block_refs = refs[:experts]
    out_ref, gate_out_ref, scaled_ref = refs[experts:]
    tokens, width = values_ref.shape
    chunk = chunk_of(width)
    chosen, rank, named = members(plane_ref[0], routes_ref[...], experts)
    hits = [slots_of(chosen, rank, d, slots) for d in range(experts)]
    picks = [hit.astype(F32).astype(BF16) for hit in hits]
    inverse = norm_factor(values_ref, chunk)

    terms = []
    for named_k in named:
        total = jnp.zeros((LANES, tokens), F32)
        for d in range(experts):
            mine = jnp.where(named_k[d : d + 1, :], hits[d].astype(F32), 0.0).astype(BF16)
            total = total + dot_rows(block_refs[d][:, width:], mine)
        terms.append(total[0:1] + total[LANES // 2 : LANES // 2 + 1])
    gate_out_ref[...] = jnp.concatenate(terms, axis=0) / gates_ref[...].astype(F32)

    def first(i, carry):
        cols = pl.ds(pl.multiple_of(i * chunk, chunk), chunk)
        grads = sum(dot_rows(picks[d], block_refs[d][:, cols]) for d in range(experts))
        grads = grads * gain_ref[:, cols]
        scaled_ref[:, cols] = grads
        normed = values_ref[:, cols].astype(F32) * inverse
        return carry + jnp.sum(grads * normed, axis=1, keepdims=True)

    mean = lax.fori_loop(0, width // chunk, first, jnp.zeros((tokens, 1), F32), unroll=True) * (1.0 / width)

    def second(i, carry):
        cols = pl.ds(pl.multiple_of(i * chunk, chunk), chunk)
        normed = values_ref[:, cols].astype(F32) * inverse
        out_ref[:, cols] = (
            cot_ref[:, cols].astype(F32) + inverse * (scaled_ref[:, cols] - normed * mean)
        ).astype(BF16)
        return carry

    lax.fori_loop(0, width // chunk, second, 0, unroll=True)


SMEM_SPEC = pl.BlockSpec(memory_space=pltpu.SMEM)
VMEM_SPEC = pl.BlockSpec(memory_space=pltpu.VMEM)


def call(body, out_shapes, args, name, scratch=(), scalars=0, hint=HINT):
    return pl.pallas_call(
        body,
        out_shape=[jax.ShapeDtypeStruct(shape, dtype) for shape, dtype in out_shapes],
        in_specs=[SMEM_SPEC] * scalars + [VMEM_SPEC] * (len(args) - scalars),
        out_specs=[VMEM_SPEC] * len(out_shapes),
        scratch_shapes=list(scratch),
        cost_estimate=hint,
        compiler_params=pltpu.CompilerParams(vmem_limit_bytes=12 << 20),
        name=name,
    )(*args)


def weight_grads(rows, cots, acts, gates, ups):
    count, width = rows[0].shape
    units = acts[0].shape[1]
    chunk = chunk_of(width)
    whole = pl.BlockSpec((count, units), lambda i: (0, 0))
    return pl.pallas_call(
        weight_kernel,
        grid=(width // chunk,),
        out_shape=[
            jax.ShapeDtypeStruct((width, units), BF16),
            jax.ShapeDtypeStruct((width, units), BF16),
            jax.ShapeDtypeStruct((units, width), BF16),
        ],
        in_specs=[pl.BlockSpec((count, chunk), lambda i: (0, i))] * 4 + [whole] * 6,
        out_specs=[
            pl.BlockSpec((chunk, units), lambda i: (i, 0)),
            pl.BlockSpec((chunk, units), lambda i: (i, 0)),
            pl.BlockSpec((units, chunk), lambda i: (0, i)),
        ],
        cost_estimate=HINT,
        compiler_params=pltpu.CompilerParams(vmem_limit_bytes=20 << 20),
        name="weight_grads",
    )(*rows, *cots, *acts, *gates, *ups)


def after(values, *earlier):
    return lax.optimization_barrier((tuple(values), tuple(earlier)))[0]


def join_kernel(pieces, *refs):
    in_refs, out_refs, sems = refs[: -len(pieces) - 1], refs[-len(pieces) - 1 : -1], refs[-1]
    copies, k = [], 0
    for out_ref, parts in zip(out_refs, pieces):
        row = 0
        for source, start, count in parts:
            copies.append(
                pltpu.make_async_copy(
                    in_refs[source].at[pl.ds(start, count)],
                    out_ref.at[pl.ds(row, count)],
                    sems.at[k],
                )
            )
            row += count
            k += 1
    for copy in copies:
        copy.start()
    for copy in copies:
        copy.wait()


def join(arrays, pieces, name):
    width = arrays[0].shape[1]
    pieces = tuple(tuple(parts) for parts in pieces)
    return pl.pallas_call(
        functools.partial(join_kernel, pieces),
        out_shape=[
            jax.ShapeDtypeStruct((sum(part[2] for part in parts), width), BF16)
            for parts in pieces
        ],
        in_specs=[pl.BlockSpec(memory_space=pl.ANY)] * len(arrays),
        out_specs=[VMEM_SPEC] * len(pieces),
        scratch_shapes=[pltpu.SemaphoreType.DMA((sum(len(parts) for parts in pieces),))],
        cost_estimate=HINT,
        compiler_params=pltpu.CompilerParams(vmem_limit_bytes=4 << 20),
        name=name,
    )(*arrays)


def part_of(own, partner, index, slots):
    rows = slice(index * slots, (index + 1) * slots)
    return own[rows].astype(F32) + partner[rows].astype(F32)


def on_device(
    fwd_input,
    fwd_routes,
    fwd_gates,
    bwd_input,
    bwd_routes,
    bwd_gates,
    out_grad,
    norm_gain,
    gate_weight,
    up_weight,
    down_weight,
):
    devices = lax.axis_size("expert")
    experts = devices // UNIT_SPLIT_COUNT
    tokens, width = fwd_input.shape[1:]
    picks = fwd_routes.shape[2]
    capacity = min(tokens, tokens * picks * 5 // (4 * experts))
    slots = -(-capacity // 8) * 8
    plane = (lax.axis_index("expert") // UNIT_SPLIT_COUNT).astype(jnp.int32).reshape(1)
    gate_matrix, up_matrix, down_matrix = gate_weight[0], up_weight[0], down_weight[0]
    units = gate_matrix.shape[1]
    fwd_ids, bwd_ids = fwd_routes[0].T, bwd_routes[0].T
    fwd_g, bwd_g = fwd_gates[0].T, bwd_gates[0].T

    fwd_blocks = call(
        functools.partial(select_norm_kernel, experts, slots),
        [((slots, width), BF16)] * experts,
        (plane, fwd_ids, fwd_input[0], norm_gain),
        "select_fwd",
        scalars=1,
    )
    both = call(
        functools.partial(select_both_kernel, experts, slots),
        [((slots, width), BF16)] * (2 * experts),
        (plane, bwd_ids, bwd_g, bwd_input[0], norm_gain, out_grad[0]),
        "select_bwd",
        scalars=1,
    )
    bwd_blocks, cot_blocks = both[:experts], both[experts:]
    rows = 2 * experts * slots

    def forward(rows_in, name):
        return call(
            forward_kernel,
            [((rows, width), BF16)],
            (rows_in, gate_matrix, up_matrix, down_matrix),
            name,
        )[0]

    def hidden(rows_in, name):
        return call(
            hidden_kernel,
            [((rows, units), BF16), ((rows, units), F32), ((rows, units), F32)],
            (rows_in, gate_matrix, up_matrix),
            name,
        )

    def backward(rows_in, cot_in, made, name):
        return call(
            backward_kernel,
            [((rows, width + LANES), BF16)] + [((rows, units), BF16)] * 2 + [((1, width), F32)],
            (rows_in, cot_in, *made, gate_matrix, up_matrix, down_matrix),
            name,
        )

    away = range(1, experts)
    far = (experts - 1) * slots
    half = experts * slots

    def over_z(blocks):
        return [swap(block, d * UNIT_SPLIT_COUNT) for d, block in zip(away, blocks)]

    laid_far = [(k, 0, slots) for k in range(experts - 1)]

    def laid_own(k, first):
        return [(first, 0, slots), (first + 1, 0, far), (first + 2, k * slots, slots), (first + 3, 0, far)]

    (near,) = join(
        [fwd_blocks[0], bwd_blocks[0], cot_blocks[0]],
        [[(k, 0, slots) for k in range(3)]],
        "near_blocks",
    )
    near_crossed, fwd_landed = swap(near, 2), over_z(fwd_blocks[1:])
    *bwd_send, near_crossed = after((*bwd_blocks[1:], near_crossed), *fwd_landed)
    (fwd_far,) = join([*fwd_landed, near_crossed], [laid_far], "far_fwd")
    *bwd_send, fwd_far = after((*bwd_send, fwd_far))
    bwd_landed, fwd_far_crossed = over_z(bwd_send), swap(fwd_far, 2)
    bwd_far, fwd_own = join(
        [*bwd_landed, fwd_blocks[0], fwd_far, near_crossed, fwd_far_crossed],
        [laid_far, laid_own(0, experts - 1)],
        "far_bwd_own_fwd",
    )
    *cot_send, bwd_far, fwd_own = after((*cot_blocks[1:], bwd_far, fwd_own))
    cot_landed, bwd_far_crossed, fwd_other = over_z(cot_send), swap(bwd_far, 2), swap(fwd_own, 1)
    out_own = forward(fwd_own, "forward_own")
    *cot_landed, bwd_far_crossed, fwd_other = after(
        (*cot_landed, bwd_far_crossed, fwd_other), out_own
    )
    cot_far, bwd_own = join(
        [*cot_landed, bwd_blocks[0], bwd_far, near_crossed, bwd_far_crossed],
        [laid_far, laid_own(1, experts - 1)],
        "far_cot_own_bwd",
    )
    cot_far, bwd_own, fwd_other = after((cot_far, bwd_own, fwd_other))
    cot_far_crossed, bwd_other = swap(cot_far, 2), swap(bwd_own, 1)
    out_other = forward(fwd_other, "forward_other")
    out_partner = swap(out_other, 1)
    made_own = hidden(bwd_own, "hidden_own")
    made_other = hidden(bwd_other, "hidden_other")
    cot_far_crossed, bwd_other, out_partner = after(
        (cot_far_crossed, bwd_other, out_partner), made_own[0], made_other[0]
    )
    (cot_own,) = join(
        [cot_blocks[0], cot_far, near_crossed, cot_far_crossed], [laid_own(2, 0)], "own_cot"
    )
    cot_own, out_partner = after((cot_own, out_partner))
    cot_other = swap(cot_own, 1)
    middle = experts // 2

    def crossing(own, partner, first, count):
        rows = slice(half + first * slots, half + (first + count) * slots)
        return (own[rows].astype(F32) + partner[rows].astype(F32)).astype(BF16)

    def home(own, partner, crossed, first):
        sums = call(
            functools.partial(add_kernel, first, slots),
            [((slots, own.shape[1]), BF16)] * middle,
            (own, partner, crossed),
            "add_columns",
            hint=None,
        )
        back = {}
        for i in range(middle)[::-1]:
            d = first + i
            back[i] = swap(sums[i], d * UNIT_SPLIT_COUNT) if d else sums[i]
        return [back[i] for i in range(middle)]

    out_high = swap(crossing(out_own, out_partner, middle, middle), 2)
    out_low = swap(crossing(out_own, out_partner, 0, middle), 2)
    norm_other, dgate_other, dup_other, gain_other = backward(
        bwd_other, cot_other, made_other, "backward_other"
    )
    norm_partner = swap(norm_other, 1)
    norm_own, dgate_own, dup_own, gain_own = backward(bwd_own, cot_own, made_own, "backward_own")
    (out_high,) = after((out_high,), norm_own)
    out_far = home(out_own, out_partner, out_high, middle)
    norm_high = swap(crossing(norm_own, norm_partner, middle, middle), 2)
    norm_low = swap(crossing(norm_own, norm_partner, 0, middle), 2)
    (dgate_own,) = after((dgate_own,), out_high, norm_partner)
    grad_gate, grad_up, grad_down = weight_grads(
        (bwd_own, bwd_other),
        (cot_own, cot_other),
        (made_own[0], made_other[0]),
        (dgate_own, dgate_other),
        (dup_own, dup_other),
    )
    held_high, out_low = after((norm_high, out_low), grad_gate)
    norm_far = home(norm_own, norm_partner, held_high, middle)
    out_near = home(out_own, out_partner, out_low, 0)
    out_back = after(out_near + out_far, held_high)
    mixed = call(
        functools.partial(mixed_kernel, experts, slots),
        [((tokens, width), BF16)],
        (plane, fwd_ids, fwd_g, fwd_input[0], *out_back),
        "mixed",
        scalars=1,
    )[0]
    low_own, low_partner, held_low = after((norm_own, norm_partner, norm_low), mixed)
    norm_near = home(low_own, low_partner, held_low, 0)
    norm_back = norm_near + norm_far
    gain_sum = gain_own + gain_other
    gain_sum = gain_sum + swap(gain_sum, 1)
    (gain_sum,) = after((gain_sum,), norm_partner)
    gain_crossed = swap(gain_sum, 2)
    gain_sum, gain_crossed = after((gain_sum, gain_crossed), mixed)
    gain_sum = gain_sum + gain_crossed
    gain_sum = sum([swap(gain_sum, d * UNIT_SPLIT_COUNT) for d in away], gain_sum)
    gain_grad = gain_sum / norm_gain

    input_grad, gate_grad = call(
        functools.partial(input_grad_kernel, experts, slots),
        [((tokens, width), BF16), ((picks, tokens), F32)],
        (plane, bwd_ids, bwd_g, bwd_input[0], out_grad[0], norm_gain, *norm_back),
        "input_grad",
        scratch=[pltpu.VMEM((tokens, width), F32)],
        scalars=1,
    )
    act_next = along_pipe(mixed, 1)
    grad_prev = along_pipe(input_grad, -1)
    return (
        act_next[None],
        grad_prev[None],
        gate_grad.T[None],
        gain_grad,
        grad_gate[None],
        grad_up[None],
        grad_down[None],
    )


def solution(mesh):
    rows = P("pipe", "expert", None)
    columns = P("pipe", None, "expert")
    return jax.shard_map(
        on_device,
        mesh=mesh,
        in_specs=(rows,) * 7 + (P("pipe", None), columns, columns, rows),
        out_specs=(rows, rows, rows, P("pipe", None), columns, columns, rows),
        check_vma=False,
    )
```
